256 devices in a mesh: group: 8 (over x, core), dev: 32 (over y, z).
Axes of the slice: x: 4, y: 4, z: 8, core: 2. Of those that a mesh axis runs over, the one named last changes fastest.
Arguments:
- queries: bfloat16 [2048, 32, 128], P(('group', 'dev')), may hold values from -0.5390625 to 0.5390625
- passages: bfloat16 [4096, 256, 128], P(('group', 'dev')), may hold values from -6 to 6
- candidates: int32 [2048, 16], P(('group', 'dev')), may hold values from 0 to 4095, as said below
- location: int32 [4096], replicated, may hold values from 0 to 4095, as said below
Outputs:
- loss: float32 [2048], P(('group', 'dev'))
- query_grad: float32 [2048, 32, 128], P(('group', 'dev'))
The draws below stay inside these ranges and needn't reach their ends.
Inputs may be any that keep to these rules, and one draw needn't show every extreme that they name: `candidates`: for each device holding queries and each device holding passage rows (rows of passages split evenly over group+dev in order), at most 2 of the sending device's pairs (query, listed document) have their document's row on that device. In every draw one device receives exactly 2 such pairs from every device. `location`: A permutation of the documents.
All inputs are finite; a program needn't handle non-finite values.
Results may differ from the reference program's by a relative error of at most 0.011.
Values may be sent and summed in bfloat16 or wider, within the bound.
A program may use at most 64 MiB of HBM per device.

```python
import jax
import jax.numpy as jnp
from jax import lax

E = 128
QT = 32
PT = 256
CAND = 16
QD = 8
PD = 16
CAP = 2
QUERIES = 2048
NPASS = 4096
DEVICES = 256


def layout(key):
    base = jax.random.fold_in(key, 7)
    key_perm, key_hot, key_order, key_local = jax.random.split(base, 4)
    location = jax.random.permutation(key_perm, NPASS).astype(jnp.int32)
    hot_target = jax.random.randint(key_hot, (), 0, DEVICES)
    slot_total = DEVICES * CAP
    pair_count = QD * CAND

    def choose_slots(one_key):
        key_first, key_second = jax.random.split(one_key)
        ranking = jax.random.permutation(key_first, slot_total).astype(jnp.int32)
        owners = jnp.arange(slot_total, dtype=jnp.int32) // CAP
        ranking = jnp.where(owners == hot_target, ranking - slot_total, ranking)
        chosen = jnp.argsort(ranking)[:pair_count].astype(jnp.int32)
        return jax.random.permutation(key_second, chosen)
    chosen = jax.vmap(choose_slots)(jax.random.split(key_order, DEVICES))
    target = chosen // CAP
    local_row = jax.random.randint(key_local, (DEVICES, pair_count), 0, PD)
    rows = (target * PD + local_row).reshape(QUERIES, CAND)
    inverse = jnp.argsort(location).astype(jnp.int32)
    return (inverse[rows].astype(jnp.int32), location)


def draw_candidates(key, part):
    return layout(key)[0]


def draw_location(key, part):
    return layout(key)[1]


def block_scale(own_key, extent, shards, low, top_value):
    gain, own = 1.0, jax.random.fold_in(own_key, 6)
    for position, shards_of in shards:
        draws = jnp.exp(jax.random.uniform(jax.random.fold_in(own, position), (shards_of,), jnp.float32, low / len(shards), top_value / len(shards)))
        gain = gain * jnp.repeat(draws, extent[position] // shards_of).reshape([-1 if axis == position else 1 for axis in range(len(extent))])
    return gain


def centred(stream_key, shape, scale, reach, cuts=(), kind=jnp.bfloat16):
    array = scale * jax.random.normal(stream_key, shape, jnp.float32)
    if cuts:
        array = array * block_scale(stream_key, shape, cuts, -0.22, 0.18)
    return jnp.clip(array, -reach, reach).astype(kind)


def setup_inputs(seed: int = 0) -> dict:
    key_list = jax.random.split(jax.random.key(seed), 5)
    queries = centred(key_list[0], (QUERIES, QT, E), 0.09, 0.5390625, ((0, 256),))
    passages = centred(key_list[1], (NPASS, PT, E), 1.0, 6.0, ((0, 256),))
    candidates = draw_candidates(jax.random.fold_in(key_list[4], 71), 0)
    location = draw_location(jax.random.fold_in(key_list[4], 71), 0)
    return {"queries": queries, "passages": passages, "candidates": candidates, "location": location}


SOFTNESS = 0.02
EPSILON = 1e-06

def normalize(values):
    floats = values.astype(jnp.float32)
    scale = lax.rsqrt(lax.optimization_barrier(jnp.sum(floats * floats, axis=-1, keepdims=True)) + EPSILON)
    return (floats * scale, scale)

def reference(queries, passages, candidates, location):
    query_unit, query_scale = normalize(queries)
    query_send = query_unit.astype(jnp.bfloat16)
    passage_unit = normalize(passages)[0].astype(jnp.bfloat16)
    rows = location[candidates].astype(jnp.int32)

    def one_block(inputs):
        query_block, row_block = inputs
        passage_block = passage_unit[row_block].astype(jnp.float32)
        logits = jnp.einsum('bqe,bkpe->bkqp', query_block.astype(jnp.float32), passage_block) / SOFTNESS
        exp_terms = jnp.exp(logits)
        token_mass = lax.optimization_barrier(jnp.sum(exp_terms, axis=-1, keepdims=True))
        pair_score = lax.optimization_barrier(jnp.sum(SOFTNESS * jnp.log(token_mass[..., 0]), axis=-1))
        attention = (exp_terms / token_mass).astype(jnp.bfloat16)
        pulled = jnp.einsum('bkqp,bkpe->bkqe', attention.astype(jnp.float32), passage_block).astype(jnp.bfloat16)
        return (pulled, pair_score)
    blocks = QUERIES // QD
    pulled, pair_score = lax.map(one_block, (query_send.reshape(blocks, QD, QT, E), rows.reshape(blocks, QD, CAND)))
    pulled = pulled.reshape(QUERIES, CAND, QT, E)
    pair_score = pair_score.reshape(QUERIES, CAND)
    exp_scores = jnp.exp(pair_score)
    total = lax.optimization_barrier(jnp.sum(exp_scores, axis=-1, keepdims=True))
    loss = jnp.log(total[:, 0]) - pair_score[:, 0]
    first = (jnp.arange(CAND) == 0).astype(jnp.float32)
    coeff = exp_scores / total - first[None, :]
    unit_grad = jnp.einsum('bk,bkqe->bqe', coeff, pulled.astype(jnp.float32))
    along = lax.optimization_barrier(jnp.sum(query_unit * unit_grad, axis=-1, keepdims=True))
    query_grad = (unit_grad - query_unit * along) * query_scale
    return (loss, query_grad)
```

```python
import jax
import jax.numpy as jnp
from jax import lax
from jax.sharding import PartitionSpec as P

SOFTNESS = 0.02
EPSILON = 1e-06


def normalize(values):
    floats = values.astype(jnp.float32)
    scale = lax.rsqrt(jnp.sum(floats * floats, axis=-1, keepdims=True) + EPSILON)
    return (floats * scale, scale)


def local(queries, passages, candidates, location):
    group_count = lax.axis_size("group")
    dev_count = lax.axis_size("dev")
    device_total = group_count * dev_count
    query_count, query_len, feat_width = queries.shape
    pass_count = passages.shape[0]
    list_len = candidates.shape[1]
    pair_count = query_count * list_len
    slot_cap = max(2, (3 * pair_count + device_total - 1) // device_total)
    slot_total = device_total * slot_cap
    query_unit, query_scale = normalize(queries)
    query_send = query_unit.astype(jnp.bfloat16)
    passage_unit = normalize(passages)[0].astype(jnp.bfloat16)
    rows = jnp.take(location, candidates.reshape(-1), axis=0)
    target = rows // pass_count
    local_row = rows % pass_count
    same_target = target[:, None] == target[None, :]
    positions = jnp.arange(pair_count, dtype=jnp.int32)
    earlier = positions[None, :] < positions[:, None]
    before = jnp.sum(same_target & earlier, axis=1)
    slot_index = target * slot_cap + before
    query_owner = positions // list_len
    outgoing = jnp.zeros((slot_total, query_len, feat_width), jnp.bfloat16)
    outgoing = outgoing.at[slot_index].set(query_send[query_owner])
    labels = (
        jnp.zeros((slot_total,), jnp.bfloat16).at[slot_index].set(local_row.astype(jnp.bfloat16))
    )
    both_axes = ("group", "dev")
    arrived = lax.all_to_all(outgoing, both_axes, split_axis=0, concat_axis=0, tiled=True)
    tags = lax.all_to_all(labels, both_axes, split_axis=0, concat_axis=0, tiled=True)
    block_rows = dev_count * slot_cap
    arrived = arrived.reshape(group_count, block_rows, query_len, feat_width)
    tags = tags.reshape(group_count, block_rows).astype(jnp.int32)

    def score_block(inputs):
        query_block, tag_block = inputs
        passage_block = jnp.take(passage_unit, tag_block, axis=0)
        logits = (
            jnp.einsum(
                "bqe,bpe->bqp", query_block, passage_block, preferred_element_type=jnp.float32
            )
            / SOFTNESS
        )
        exp_terms = jnp.exp(logits)
        token_mass = jnp.sum(exp_terms, axis=-1, keepdims=True)
        pair_score = jnp.sum(SOFTNESS * jnp.log(token_mass[..., 0]), axis=-1)
        attention = (exp_terms / token_mass).astype(jnp.bfloat16)
        pulled = jnp.einsum(
            "bqp,bpe->bqe", attention, passage_block, preferred_element_type=jnp.float32
        )
        return (pulled.astype(jnp.bfloat16), pair_score)

    pulled, scores = lax.map(score_block, (arrived, tags))
    pulled = pulled.reshape(slot_total, query_len, feat_width)
    scores = scores.reshape(slot_total)
    pulled_flat = lax.all_to_all(pulled, both_axes, split_axis=0, concat_axis=0, tiled=True)
    scores_flat = lax.all_to_all(scores, both_axes, split_axis=0, concat_axis=0, tiled=True)
    pair_pulled = jnp.take(pulled_flat, slot_index, axis=0).reshape(
        query_count, list_len, query_len, feat_width
    )
    pair_score = jnp.take(scores_flat, slot_index, axis=0).reshape(query_count, list_len)
    exp_scores = jnp.exp(pair_score)
    total = jnp.sum(exp_scores, axis=-1, keepdims=True)
    loss = jnp.log(total[:, 0]) - pair_score[:, 0]
    first = (jnp.arange(list_len) == 0).astype(jnp.float32)
    coeff = exp_scores / total - first[None, :]
    unit_grad = jnp.einsum("bk,bkqe->bqe", coeff, pair_pulled.astype(jnp.float32))
    along = jnp.sum(query_unit * unit_grad, axis=-1, keepdims=True)
    query_grad = (unit_grad - query_unit * along) * query_scale
    return (loss, query_grad)


def solution(mesh):
    placed = (
        P(("group", "dev"), None, None),
        P(("group", "dev"), None, None),
        P(("group", "dev"), None),
        P(),
    )
    return jax.shard_map(
        local,
        mesh=mesh,
        in_specs=placed,
        out_specs=(P(("group", "dev")), P(("group", "dev"), None, None)),
        check_vma=False,
    )
```

```python
import jax
import jax.numpy as jnp
from jax import lax
from jax.sharding import PartitionSpec as P

SOFTNESS = 0.02
EPSILON = 1e-06


def normalize(values):
    floats = values.astype(jnp.float32)
    scale = lax.rsqrt(jnp.sum(floats * floats, axis=-1, keepdims=True) + EPSILON)
    return (floats * scale, scale)


def local(queries, passages, candidates, location):
    group_count = lax.axis_size("group")
    dev_count = lax.axis_size("dev")
    device_total = group_count * dev_count
    query_count, query_len, feat_width = queries.shape
    pass_count = passages.shape[0]
    list_len = candidates.shape[1]
    pair_count = query_count * list_len
    slot_cap = max(2, (3 * pair_count + device_total - 1) // device_total)
    slot_total = device_total * slot_cap
    query_unit, query_scale = normalize(queries)
    query_send = query_unit.astype(jnp.bfloat16)
    passage_unit = normalize(passages)[0].astype(jnp.bfloat16)
    rows = jnp.take(location, candidates.reshape(-1), axis=0)
    target = rows // pass_count
    local_row = rows % pass_count
    same_target = target[:, None] == target[None, :]
    positions = jnp.arange(pair_count, dtype=jnp.int32)
    earlier = positions[None, :] < positions[:, None]
    before = jnp.sum(same_target & earlier, axis=1)
    slot_index = target * slot_cap + before
    token_width = query_len * feat_width
    pair_of_slot = jnp.zeros((slot_total,), jnp.int32).at[slot_index].set(positions)
    slot_owner = pair_of_slot // list_len
    slot_label = jnp.take(local_row, pair_of_slot, axis=0).astype(jnp.bfloat16)
    label_block = jnp.zeros((slot_total, feat_width), jnp.bfloat16).at[:, 0].set(slot_label)
    outgoing = jnp.concatenate(
        [jnp.take(query_send.reshape(query_count, token_width), slot_owner, axis=0), label_block],
        axis=1,
    )
    both_axes = ("group", "dev")
    arrived = lax.all_to_all(outgoing, both_axes, split_axis=0, concat_axis=0, tiled=True)
    block_rows = dev_count * slot_cap
    tags = arrived[:, token_width].astype(jnp.int32).reshape(group_count, block_rows)
    arrived = arrived[:, :token_width].reshape(group_count, block_rows, query_len, feat_width)

    def score_block(inputs):
        query_block, tag_block = inputs
        passage_block = jnp.take(passage_unit, tag_block, axis=0)
        logits = (
            jnp.einsum(
                "bqe,bpe->bqp", query_block, passage_block, preferred_element_type=jnp.float32
            )
            / SOFTNESS
        )
        exp_terms = jnp.exp(logits)
        token_mass = jnp.sum(exp_terms, axis=-1, keepdims=True)
        pair_score = jnp.sum(SOFTNESS * jnp.log(token_mass[..., 0]), axis=-1)
        attention = (exp_terms / token_mass).astype(jnp.bfloat16)
        pulled = jnp.einsum(
            "bqp,bpe->bqe", attention, passage_block, preferred_element_type=jnp.float32
        )
        score_high = pair_score.astype(jnp.bfloat16)
        score_low = (pair_score - score_high.astype(jnp.float32)).astype(jnp.bfloat16)
        score_cols = jnp.zeros((pulled.shape[0], feat_width), jnp.bfloat16)
        score_cols = score_cols.at[:, 0].set(score_high).at[:, 1].set(score_low)
        pulled_rows = pulled.astype(jnp.bfloat16).reshape(pulled.shape[0], token_width)
        return jnp.concatenate([pulled_rows, score_cols], axis=1)

    returning = lax.map(score_block, (arrived, tags)).reshape(slot_total, token_width + feat_width)
    returned = lax.all_to_all(returning, both_axes, split_axis=0, concat_axis=0, tiled=True)
    pulled_flat = returned[:, :token_width].reshape(slot_total, query_len, feat_width)
    scores_flat = returned[:, token_width].astype(jnp.float32) + returned[
        :, token_width + 1
    ].astype(jnp.float32)
    pair_pulled = jnp.take(pulled_flat, slot_index, axis=0).reshape(
        query_count, list_len, query_len, feat_width
    )
    pair_score = jnp.take(scores_flat, slot_index, axis=0).reshape(query_count, list_len)
    exp_scores = jnp.exp(pair_score)
    total = jnp.sum(exp_scores, axis=-1, keepdims=True)
    loss = jnp.log(total[:, 0]) - pair_score[:, 0]
    first = (jnp.arange(list_len) == 0).astype(jnp.float32)
    coeff = exp_scores / total - first[None, :]
    unit_grad = jnp.einsum("bk,bkqe->bqe", coeff, pair_pulled.astype(jnp.float32))
    along = jnp.sum(query_unit * unit_grad, axis=-1, keepdims=True)
    query_grad = (unit_grad - query_unit * along) * query_scale
    return (loss, query_grad)


def solution(mesh):
    placed = (
        P(("group", "dev"), None, None),
        P(("group", "dev"), None, None),
        P(("group", "dev"), None),
        P(),
    )
    return jax.shard_map(
        local,
        mesh=mesh,
        in_specs=placed,
        out_specs=(P(("group", "dev")), P(("group", "dev"), None, None)),
        check_vma=False,
    )
```

```python
import jax
import jax.numpy as jnp
from jax import lax
from jax.sharding import PartitionSpec as P

SOFTNESS = 0.02
EPSILON = 1e-06


def normalize(values):
    floats = values.astype(jnp.float32)
    scale = lax.rsqrt(jnp.sum(floats * floats, axis=-1, keepdims=True) + EPSILON)
    return (floats * scale, scale)


def local(queries, passages, candidates, location):
    group_count = lax.axis_size("group")
    dev_count = lax.axis_size("dev")
    device_total = group_count * dev_count
    query_count, query_len, feat_width = queries.shape
    pass_count = passages.shape[0]
    list_len = candidates.shape[1]
    pair_count = query_count * list_len
    slot_cap = max(2, (3 * pair_count + device_total - 1) // device_total)
    slot_total = device_total * slot_cap
    query_unit, query_scale = normalize(queries)
    query_send = query_unit.astype(jnp.bfloat16)
    passage_unit = normalize(passages)[0].astype(jnp.bfloat16)
    rows = jnp.take(location, candidates.reshape(-1), axis=0)
    target = rows // pass_count
    local_row = rows % pass_count
    same_target = target[:, None] == target[None, :]
    positions = jnp.arange(pair_count, dtype=jnp.int32)
    earlier = positions[None, :] < positions[:, None]
    before = jnp.sum(same_target & earlier, axis=1)
    slot_index = target * slot_cap + before
    pair_of_slot = jnp.zeros((slot_total,), jnp.int32).at[slot_index].set(positions)
    outgoing = jnp.take(query_send, pair_of_slot // list_len, axis=0)
    labels = jnp.take(local_row, pair_of_slot, axis=0).astype(jnp.bfloat16)
    both_axes = ("group", "dev")
    outgoing = outgoing.reshape(device_total, slot_cap, query_len, feat_width)
    labels = labels.reshape(device_total, slot_cap)
    tags = lax.all_to_all(labels, both_axes, split_axis=0, concat_axis=0, tiled=True)
    tags = tags.astype(jnp.int32)
    block_rows = 64

    def score_block(inputs):
        query_block, tag_block = inputs
        passage_block = jnp.take(passage_unit, tag_block, axis=0)
        logits = (
            jnp.einsum(
                "bqe,bpe->bqp", query_block, passage_block, preferred_element_type=jnp.float32
            )
            / SOFTNESS
        )
        exp_terms = jnp.exp(logits)
        token_mass = jnp.sum(exp_terms, axis=-1, keepdims=True)
        pair_score = jnp.sum(SOFTNESS * jnp.log(token_mass[..., 0]), axis=-1)
        attention = (exp_terms / token_mass).astype(jnp.bfloat16)
        pulled = jnp.einsum(
            "bqp,bpe->bqe", attention, passage_block, preferred_element_type=jnp.float32
        )
        return (pulled.astype(jnp.bfloat16), pair_score)

    returned = []
    scores = []
    for slot in range(slot_cap):
        arrived = lax.all_to_all(
            outgoing[:, slot], both_axes, split_axis=0, concat_axis=0, tiled=True
        )
        blocks = device_total // block_rows
        pulled, score = lax.map(
            score_block,
            (
                arrived.reshape(blocks, block_rows, query_len, feat_width),
                tags[:, slot].reshape(blocks, block_rows),
            ),
        )
        pulled = pulled.reshape(device_total, query_len, feat_width)
        returned.append(lax.all_to_all(pulled, both_axes, split_axis=0, concat_axis=0, tiled=True))
        scores.append(score.reshape(device_total))
    scores = jnp.stack(scores, axis=1)
    scores_flat = lax.all_to_all(scores, both_axes, split_axis=0, concat_axis=0, tiled=True)
    pair_score = jnp.take(scores_flat.reshape(slot_total), slot_index, axis=0).reshape(
        query_count, list_len
    )
    pair_pulled = jnp.take(returned[0], target, axis=0)
    for slot in range(1, slot_cap):
        pair_pulled = jnp.where(
            (before == slot)[:, None, None], jnp.take(returned[slot], target, axis=0), pair_pulled
        )
    pair_pulled = pair_pulled.reshape(query_count, list_len, query_len, feat_width)
    exp_scores = jnp.exp(pair_score)
    total = jnp.sum(exp_scores, axis=-1, keepdims=True)
    loss = jnp.log(total[:, 0]) - pair_score[:, 0]
    first = (jnp.arange(list_len) == 0).astype(jnp.float32)
    coeff = exp_scores / total - first[None, :]
    unit_grad = jnp.einsum("bk,bkqe->bqe", coeff, pair_pulled.astype(jnp.float32))
    along = jnp.sum(query_unit * unit_grad, axis=-1, keepdims=True)
    query_grad = (unit_grad - query_unit * along) * query_scale
    return (loss, query_grad)


def solution(mesh):
    placed = (
        P(("group", "dev"), None, None),
        P(("group", "dev"), None, None),
        P(("group", "dev"), None),
        P(),
    )
    return jax.shard_map(
        local,
        mesh=mesh,
        in_specs=placed,
        out_specs=(P(("group", "dev")), P(("group", "dev"), None, None)),
        check_vma=False,
    )
```

```python
import jax
import jax.numpy as jnp
from jax import lax
from jax.sharding import PartitionSpec as P

SOFTNESS = 0.02
EPSILON = 1e-06


def normalize(values):
    floats = values.astype(jnp.float32)
    scale = lax.rsqrt(jnp.sum(floats * floats, axis=-1, keepdims=True) + EPSILON)
    return (floats * scale, scale)


def local(queries, passages, candidates, location):
    group_count = lax.axis_size("group")
    dev_count = lax.axis_size("dev")
    device_total = group_count * dev_count
    query_count, query_len, feat_width = queries.shape
    pass_count = passages.shape[0]
    list_len = candidates.shape[1]
    pair_count = query_count * list_len
    slot_cap = max(2, (3 * pair_count + device_total - 1) // device_total)
    slot_total = device_total * slot_cap
    query_unit, query_scale = normalize(queries)
    query_send = query_unit.astype(jnp.bfloat16)
    passage_unit = normalize(passages)[0].astype(jnp.bfloat16)
    rows = jnp.take(location, candidates.reshape(-1), axis=0)
    target = rows // pass_count
    local_row = rows % pass_count
    same_target = target[:, None] == target[None, :]
    positions = jnp.arange(pair_count, dtype=jnp.int32)
    earlier = positions[None, :] < positions[:, None]
    before = jnp.sum(same_target & earlier, axis=1)
    slot_index = target * slot_cap + before
    pair_of_slot = jnp.zeros((slot_total,), jnp.int32).at[slot_index].set(positions)
    outgoing = jnp.take(query_send, pair_of_slot // list_len, axis=0)
    labels = jnp.take(local_row, pair_of_slot, axis=0).astype(jnp.bfloat16)
    both_axes = ("group", "dev")
    outgoing = outgoing.reshape(device_total, slot_cap, query_len, feat_width)
    labels = labels.reshape(device_total, slot_cap)
    me = lax.axis_index("group") * dev_count + lax.axis_index("dev")
    all_labels = lax.all_gather(labels, both_axes, axis=0, tiled=False)
    tags = lax.dynamic_index_in_dim(all_labels, me, axis=1, keepdims=False).astype(jnp.int32)
    block_rows = 64

    def score_block(inputs):
        query_block, tag_block = inputs
        passage_block = jnp.take(passage_unit, tag_block, axis=0)
        logits = (
            jnp.einsum(
                "bqe,bpe->bqp", query_block, passage_block, preferred_element_type=jnp.float32
            )
            / SOFTNESS
        )
        exp_terms = jnp.exp(logits)
        token_mass = jnp.sum(exp_terms, axis=-1, keepdims=True)
        pair_score = jnp.sum(SOFTNESS * jnp.log(token_mass[..., 0]), axis=-1)
        attention = (exp_terms / token_mass).astype(jnp.bfloat16)
        pulled = jnp.einsum(
            "bqp,bpe->bqe", attention, passage_block, preferred_element_type=jnp.float32
        )
        return (pulled.astype(jnp.bfloat16), pair_score)

    returned = []
    scores = []
    for slot in range(slot_cap):
        arrived = lax.all_to_all(
            outgoing[:, slot], both_axes, split_axis=0, concat_axis=0, tiled=True
        )
        blocks = device_total // block_rows
        pulled, score = lax.map(
            score_block,
            (
                arrived.reshape(blocks, block_rows, query_len, feat_width),
                tags[:, slot].reshape(blocks, block_rows),
            ),
        )
        pulled = pulled.reshape(device_total, query_len, feat_width)
        returned.append(lax.all_to_all(pulled, both_axes, split_axis=0, concat_axis=0, tiled=True))
        scores.append(score.reshape(device_total))
    scores = jnp.stack(scores, axis=1)
    all_scores = lax.all_gather(scores, both_axes, axis=0, tiled=False)
    scores_flat = lax.dynamic_index_in_dim(all_scores, me, axis=1, keepdims=False)
    pair_score = jnp.take(scores_flat.reshape(slot_total), slot_index, axis=0).reshape(
        query_count, list_len
    )
    pair_pulled = jnp.take(returned[0], target, axis=0)
    for slot in range(1, slot_cap):
        pair_pulled = jnp.where(
            (before == slot)[:, None, None], jnp.take(returned[slot], target, axis=0), pair_pulled
        )
    pair_pulled = pair_pulled.reshape(query_count, list_len, query_len, feat_width)
    exp_scores = jnp.exp(pair_score)
    total = jnp.sum(exp_scores, axis=-1, keepdims=True)
    loss = jnp.log(total[:, 0]) - pair_score[:, 0]
    first = (jnp.arange(list_len) == 0).astype(jnp.float32)
    coeff = exp_scores / total - first[None, :]
    unit_grad = jnp.einsum("bk,bkqe->bqe", coeff, pair_pulled.astype(jnp.float32))
    along = jnp.sum(query_unit * unit_grad, axis=-1, keepdims=True)
    query_grad = (unit_grad - query_unit * along) * query_scale
    return (loss, query_grad)


def solution(mesh):
    placed = (
        P(("group", "dev"), None, None),
        P(("group", "dev"), None, None),
        P(("group", "dev"), None),
        P(),
    )
    return jax.shard_map(
        local,
        mesh=mesh,
        in_specs=placed,
        out_specs=(P(("group", "dev")), P(("group", "dev"), None, None)),
        check_vma=False,
    )
```

```python
import jax
import jax.numpy as jnp
from jax import lax
from jax.sharding import PartitionSpec as P

SOFTNESS = 0.02
EPSILON = 1e-06


def normalize(values):
    floats = values.astype(jnp.float32)
    scale = lax.rsqrt(jnp.sum(floats * floats, axis=-1, keepdims=True) + EPSILON)
    return (floats * scale, scale)


def local(queries, passages, candidates, location):
    group_count = lax.axis_size("group")
    dev_count = lax.axis_size("dev")
    device_total = group_count * dev_count
    query_count, query_len, feat_width = queries.shape
    pass_count = passages.shape[0]
    list_len = candidates.shape[1]
    pair_count = query_count * list_len
    slot_cap = max(2, (3 * pair_count + device_total - 1) // device_total)
    slot_total = device_total * slot_cap
    query_unit, query_scale = normalize(queries)
    query_send = query_unit.astype(jnp.bfloat16)
    passage_unit = normalize(passages)[0].astype(jnp.bfloat16)
    rows = jnp.take(location, candidates.reshape(-1), axis=0)
    target = rows // pass_count
    local_row = rows % pass_count
    same_target = target[:, None] == target[None, :]
    positions = jnp.arange(pair_count, dtype=jnp.int32)
    earlier = positions[None, :] < positions[:, None]
    before = jnp.sum(same_target & earlier, axis=1)
    slot_index = target * slot_cap + before
    pair_of_slot = jnp.zeros((slot_total,), jnp.int32).at[slot_index].set(positions)
    outgoing = jnp.take(query_send, pair_of_slot // list_len, axis=0)
    labels = jnp.take(local_row, pair_of_slot, axis=0).astype(jnp.bfloat16)
    both_axes = ("group", "dev")
    outgoing = outgoing.reshape(device_total, slot_cap, query_len, feat_width)
    labels = labels.reshape(device_total, slot_cap)
    tags = lax.all_to_all(labels, both_axes, split_axis=0, concat_axis=0, tiled=True)
    tags = tags.astype(jnp.int32)
    block_rows = 64

    def score_block(inputs):
        query_block, tag_block = inputs
        passage_block = jnp.take(passage_unit, tag_block, axis=0)
        logits = (
            jnp.einsum(
                "bqe,bpe->bqp", query_block, passage_block, preferred_element_type=jnp.float32
            )
            / SOFTNESS
        )
        exp_terms = jnp.exp(logits)
        token_mass = jnp.sum(exp_terms, axis=-1, keepdims=True)
        pair_score = jnp.sum(SOFTNESS * jnp.log(token_mass[..., 0]), axis=-1)
        attention = (exp_terms / token_mass).astype(jnp.bfloat16)
        pulled = jnp.einsum(
            "bqp,bpe->bqe", attention, passage_block, preferred_element_type=jnp.float32
        )
        return (pulled.astype(jnp.bfloat16), pair_score)

    returned = []
    scores = []
    for slot in range(slot_cap):
        arrived = lax.all_to_all(
            outgoing[:, slot], both_axes, split_axis=0, concat_axis=0, tiled=True
        )
        blocks = device_total // block_rows
        pulled, score = lax.map(
            score_block,
            (
                arrived.reshape(blocks, block_rows, query_len, feat_width),
                tags[:, slot].reshape(blocks, block_rows),
            ),
        )
        pulled = pulled.reshape(device_total, query_len, feat_width)
        returned.append(lax.all_to_all(pulled, both_axes, split_axis=0, concat_axis=0, tiled=True))
        scores.append(score.reshape(device_total))
    scores = jnp.stack(scores, axis=1)
    scores, returned[-1] = lax.optimization_barrier((scores, returned[-1]))
    scores_flat = lax.all_to_all(scores, both_axes, split_axis=0, concat_axis=0, tiled=True)
    pair_score = jnp.take(scores_flat.reshape(slot_total), slot_index, axis=0).reshape(
        query_count, list_len
    )
    pair_pulled = jnp.take(returned[0], target, axis=0)
    for slot in range(1, slot_cap):
        pair_pulled = jnp.where(
            (before == slot)[:, None, None], jnp.take(returned[slot], target, axis=0), pair_pulled
        )
    pair_pulled = pair_pulled.reshape(query_count, list_len, query_len, feat_width)
    exp_scores = jnp.exp(pair_score)
    total = jnp.sum(exp_scores, axis=-1, keepdims=True)
    loss = jnp.log(total[:, 0]) - pair_score[:, 0]
    first = (jnp.arange(list_len) == 0).astype(jnp.float32)
    coeff = exp_scores / total - first[None, :]
    unit_grad = jnp.einsum("bk,bkqe->bqe", coeff, pair_pulled.astype(jnp.float32))
    along = jnp.sum(query_unit * unit_grad, axis=-1, keepdims=True)
    query_grad = (unit_grad - query_unit * along) * query_scale
    return (loss, query_grad)


def solution(mesh):
    placed = (
        P(("group", "dev"), None, None),
        P(("group", "dev"), None, None),
        P(("group", "dev"), None),
        P(),
    )
    return jax.shard_map(
        local,
        mesh=mesh,
        in_specs=placed,
        out_specs=(P(("group", "dev")), P(("group", "dev"), None, None)),
        check_vma=False,
    )
```

```python
import jax
import jax.numpy as jnp
from jax import lax
from jax.sharding import PartitionSpec as P

SOFTNESS = 0.02
EPSILON = 1e-06


def normalize(values):
    floats = values.astype(jnp.float32)
    scale = lax.rsqrt(jnp.sum(floats * floats, axis=-1, keepdims=True) + EPSILON)
    return (floats * scale, scale)


def local(queries, passages, candidates, location):
    group_count = lax.axis_size("group")
    dev_count = lax.axis_size("dev")
    device_total = group_count * dev_count
    query_count, query_len, feat_width = queries.shape
    pass_count = passages.shape[0]
    list_len = candidates.shape[1]
    pair_count = query_count * list_len
    slot_cap = max(2, (3 * pair_count + device_total - 1) // device_total)
    slot_total = device_total * slot_cap
    query_unit, query_scale = normalize(queries)
    query_send = query_unit.astype(jnp.bfloat16)
    passage_unit = normalize(passages)[0].astype(jnp.bfloat16)
    rows = jnp.take(location, candidates.reshape(-1), axis=0)
    target = rows // pass_count
    local_row = rows % pass_count
    same_target = target[:, None] == target[None, :]
    positions = jnp.arange(pair_count, dtype=jnp.int32)
    earlier = positions[None, :] < positions[:, None]
    before = jnp.sum(same_target & earlier, axis=1)
    slot_index = target * slot_cap + before
    pair_of_slot = jnp.zeros((slot_total,), jnp.int32).at[slot_index].set(positions)
    outgoing = jnp.take(query_send, pair_of_slot // list_len, axis=0)
    labels = jnp.take(local_row, pair_of_slot, axis=0).astype(jnp.bfloat16)
    both_axes = ("group", "dev")
    outgoing = outgoing.reshape(device_total, slot_cap, query_len, feat_width)
    labels = labels.reshape(device_total, slot_cap)
    me = lax.axis_index("group") * dev_count + lax.axis_index("dev")
    mine = (jnp.arange(device_total) == me)[None, :, None]
    tags = lax.psum_scatter(
        jnp.where(mine, labels[:, None, :], 0).astype(jnp.bfloat16),
        both_axes,
        scatter_dimension=0,
        tiled=True,
    )
    tags = tags.reshape(device_total, slot_cap).astype(jnp.int32)
    block_rows = 64

    def score_block(inputs):
        query_block, tag_block = inputs
        passage_block = jnp.take(passage_unit, tag_block, axis=0)
        logits = (
            jnp.einsum(
                "bqe,bpe->bqp", query_block, passage_block, preferred_element_type=jnp.float32
            )
            / SOFTNESS
        )
        exp_terms = jnp.exp(logits)
        token_mass = jnp.sum(exp_terms, axis=-1, keepdims=True)
        pair_score = jnp.sum(SOFTNESS * jnp.log(token_mass[..., 0]), axis=-1)
        attention = (exp_terms / token_mass).astype(jnp.bfloat16)
        pulled = jnp.einsum(
            "bqp,bpe->bqe", attention, passage_block, preferred_element_type=jnp.float32
        )
        return (pulled.astype(jnp.bfloat16), pair_score)

    returned = []
    scores = []
    for slot in range(slot_cap):
        arrived = lax.all_to_all(
            outgoing[:, slot], both_axes, split_axis=0, concat_axis=0, tiled=True
        )
        blocks = device_total // block_rows
        pulled, score = lax.map(
            score_block,
            (
                arrived.reshape(blocks, block_rows, query_len, feat_width),
                tags[:, slot].reshape(blocks, block_rows),
            ),
        )
        pulled = pulled.reshape(device_total, query_len, feat_width)
        returned.append(lax.all_to_all(pulled, both_axes, split_axis=0, concat_axis=0, tiled=True))
        scores.append(score.reshape(device_total))
    scores = jnp.stack(scores, axis=1)
    scores, returned[-1] = lax.optimization_barrier((scores, returned[-1]))
    scores_flat = lax.psum_scatter(
        jnp.where(mine, scores[:, None, :], 0.0), both_axes, scatter_dimension=0, tiled=True
    )
    pair_score = jnp.take(scores_flat.reshape(slot_total), slot_index, axis=0).reshape(
        query_count, list_len
    )
    pair_pulled = jnp.take(returned[0], target, axis=0)
    for slot in range(1, slot_cap):
        pair_pulled = jnp.where(
            (before == slot)[:, None, None], jnp.take(returned[slot], target, axis=0), pair_pulled
        )
    pair_pulled = pair_pulled.reshape(query_count, list_len, query_len, feat_width)
    exp_scores = jnp.exp(pair_score)
    total = jnp.sum(exp_scores, axis=-1, keepdims=True)
    loss = jnp.log(total[:, 0]) - pair_score[:, 0]
    first = (jnp.arange(list_len) == 0).astype(jnp.float32)
    coeff = exp_scores / total - first[None, :]
    unit_grad = jnp.einsum("bk,bkqe->bqe", coeff, pair_pulled.astype(jnp.float32))
    along = jnp.sum(query_unit * unit_grad, axis=-1, keepdims=True)
    query_grad = (unit_grad - query_unit * along) * query_scale
    return (loss, query_grad)


def solution(mesh):
    placed = (
        P(("group", "dev"), None, None),
        P(("group", "dev"), None, None),
        P(("group", "dev"), None),
        P(),
    )
    return jax.shard_map(
        local,
        mesh=mesh,
        in_specs=placed,
        out_specs=(P(("group", "dev")), P(("group", "dev"), None, None)),
        check_vma=False,
    )
```

```python
import functools

import jax
import jax.numpy as jnp
from jax import lax
from jax.experimental import pallas as pl
from jax.experimental.pallas import tpu as pltpu
from jax.sharding import PartitionSpec as P

MESH = pl.DeviceIdType.MESH

SOFTNESS = 0.02
EPSILON = 1e-06


def normalize(values):
    floats = values.astype(jnp.float32)
    scale = lax.rsqrt(jnp.sum(floats * floats, axis=-1, keepdims=True) + EPSILON)
    return (floats * scale, scale)


def exchange_kernel(dev_count, rows_ref, out_ref, landing, send_sem, recv_sem):
    total = rows_ref.shape[0]
    me = lax.axis_index("group") * dev_count + lax.axis_index("dev")

    def peer_id(step):
        peer = lax.rem(me + step, total)
        return peer, (lax.div(peer, dev_count), lax.rem(peer, dev_count))

    barrier = pltpu.get_barrier_semaphore()

    def greet(step, carry):
        pl.semaphore_signal(barrier, inc=1, device_id=peer_id(step)[1], device_id_type=MESH)
        return carry

    lax.fori_loop(1, total, greet, 0)
    pl.semaphore_wait(barrier, total - 1)

    def send(step, carry):
        peer, device = peer_id(step)
        pltpu.make_async_remote_copy(
            src_ref=rows_ref.at[pl.ds(peer, 1)],
            dst_ref=landing.at[pl.ds(me, 1)],
            send_sem=send_sem,
            recv_sem=recv_sem,
            device_id=device,
            device_id_type=MESH,
        ).start()
        return carry

    lax.fori_loop(1, total, send, 0)
    landing[pl.ds(me, 1), :] = rows_ref[pl.ds(me, 1), :]
    every = pltpu.make_async_remote_copy(
        src_ref=rows_ref.at[pl.ds(0, total - 1)],
        dst_ref=landing.at[pl.ds(0, total - 1)],
        send_sem=send_sem,
        recv_sem=recv_sem,
        device_id=peer_id(1)[1],
        device_id_type=MESH,
    )
    every.wait_send()
    every.wait_recv()
    out_ref[...] = landing[...]


def exchange(rows, dev_count, tag):
    return pl.pallas_call(
        functools.partial(exchange_kernel, dev_count),
        out_shape=jax.ShapeDtypeStruct(rows.shape, rows.dtype),
        in_specs=[pl.BlockSpec(memory_space=pltpu.VMEM)],
        out_specs=pl.BlockSpec(memory_space=pltpu.VMEM),
        scratch_shapes=[
            pltpu.VMEM(rows.shape, rows.dtype),
            pltpu.SemaphoreType.DMA(()),
            pltpu.SemaphoreType.DMA(()),
        ],
        compiler_params=pltpu.CompilerParams(collective_id=tag, has_side_effects=True),
    )(rows)


def widen(small, feat_width):
    return jnp.pad(small.astype(jnp.float32), ((0, 0), (0, feat_width - small.shape[1])))


def local(queries, passages, candidates, location):
    group_count = lax.axis_size("group")
    dev_count = lax.axis_size("dev")
    device_total = group_count * dev_count
    query_count, query_len, feat_width = queries.shape
    pass_count = passages.shape[0]
    list_len = candidates.shape[1]
    pair_count = query_count * list_len
    slot_cap = max(2, (3 * pair_count + device_total - 1) // device_total)
    slot_total = device_total * slot_cap
    query_unit, query_scale = normalize(queries)
    query_send = query_unit.astype(jnp.bfloat16)
    passage_unit = normalize(passages)[0].astype(jnp.bfloat16)
    rows = jnp.take(location, candidates.reshape(-1), axis=0)
    target = rows // pass_count
    local_row = rows % pass_count
    same_target = target[:, None] == target[None, :]
    positions = jnp.arange(pair_count, dtype=jnp.int32)
    earlier = positions[None, :] < positions[:, None]
    before = jnp.sum(same_target & earlier, axis=1)
    slot_index = target * slot_cap + before
    pair_of_slot = jnp.zeros((slot_total,), jnp.int32).at[slot_index].set(positions)
    outgoing = jnp.take(query_send, pair_of_slot // list_len, axis=0)
    labels = jnp.take(local_row, pair_of_slot, axis=0).astype(jnp.bfloat16)
    both_axes = ("group", "dev")
    outgoing = outgoing.reshape(device_total, slot_cap, query_len, feat_width)
    labels = labels.reshape(device_total, slot_cap)
    tags = exchange(widen(labels, feat_width), dev_count, 0)[:, :slot_cap].astype(jnp.int32)
    block_rows = 64

    def score_block(inputs):
        query_block, tag_block = inputs
        passage_block = jnp.take(passage_unit, tag_block, axis=0)
        logits = (
            jnp.einsum(
                "bqe,bpe->bqp", query_block, passage_block, preferred_element_type=jnp.float32
            )
            / SOFTNESS
        )
        exp_terms = jnp.exp(logits)
        token_mass = jnp.sum(exp_terms, axis=-1, keepdims=True)
        pair_score = jnp.sum(SOFTNESS * jnp.log(token_mass[..., 0]), axis=-1)
        attention = (exp_terms / token_mass).astype(jnp.bfloat16)
        pulled = jnp.einsum(
            "bqp,bpe->bqe", attention, passage_block, preferred_element_type=jnp.float32
        )
        return (pulled.astype(jnp.bfloat16), pair_score)

    returned = []
    scores = []
    for slot in range(slot_cap):
        arrived = lax.all_to_all(
            outgoing[:, slot], both_axes, split_axis=0, concat_axis=0, tiled=True
        )
        blocks = device_total // block_rows
        pulled, score = lax.map(
            score_block,
            (
                arrived.reshape(blocks, block_rows, query_len, feat_width),
                tags[:, slot].reshape(blocks, block_rows),
            ),
        )
        pulled = pulled.reshape(device_total, query_len, feat_width)
        returned.append(lax.all_to_all(pulled, both_axes, split_axis=0, concat_axis=0, tiled=True))
        scores.append(score.reshape(device_total))
    scores = jnp.stack(scores, axis=1)
    scores, returned[-1] = lax.optimization_barrier((scores, returned[-1]))
    scores_flat = exchange(widen(scores, feat_width), dev_count, 1)[:, :slot_cap]
    pair_score = jnp.take(scores_flat.reshape(slot_total), slot_index, axis=0).reshape(
        query_count, list_len
    )
    pair_pulled = jnp.take(returned[0], target, axis=0)
    for slot in range(1, slot_cap):
        pair_pulled = jnp.where(
            (before == slot)[:, None, None], jnp.take(returned[slot], target, axis=0), pair_pulled
        )
    pair_pulled = pair_pulled.reshape(query_count, list_len, query_len, feat_width)
    exp_scores = jnp.exp(pair_score)
    total = jnp.sum(exp_scores, axis=-1, keepdims=True)
    loss = jnp.log(total[:, 0]) - pair_score[:, 0]
    first = (jnp.arange(list_len) == 0).astype(jnp.float32)
    coeff = exp_scores / total - first[None, :]
    unit_grad = jnp.einsum("bk,bkqe->bqe", coeff, pair_pulled.astype(jnp.float32))
    along = jnp.sum(query_unit * unit_grad, axis=-1, keepdims=True)
    query_grad = (unit_grad - query_unit * along) * query_scale
    return (loss, query_grad)


def solution(mesh):
    placed = (
        P(("group", "dev"), None, None),
        P(("group", "dev"), None, None),
        P(("group", "dev"), None),
        P(),
    )
    return jax.shard_map(
        local,
        mesh=mesh,
        in_specs=placed,
        out_specs=(P(("group", "dev")), P(("group", "dev"), None, None)),
        check_vma=False,
    )
```

```python
import functools

import jax
import jax.numpy as jnp
from jax import lax
from jax.experimental import pallas as pl
from jax.experimental.pallas import tpu as pltpu
from jax.sharding import PartitionSpec as P

MESH = pl.DeviceIdType.MESH

SOFTNESS = 0.02
EPSILON = 1e-06


def normalize(values):
    floats = values.astype(jnp.float32)
    scale = lax.rsqrt(jnp.sum(floats * floats, axis=-1, keepdims=True) + EPSILON)
    return (floats * scale, scale)


def exchange_kernel(dev_count, count, *refs):
    sources, targets = refs[:count], refs[count : 2 * count]
    landings = refs[2 * count : 3 * count]
    send_sems, recv_sems = refs[3 * count], refs[3 * count + 1]
    total = sources[0].shape[0]
    me = lax.axis_index("group") * dev_count + lax.axis_index("dev")

    def peer_id(step):
        peer = lax.rem(me + step, total)
        return peer, (lax.div(peer, dev_count), lax.rem(peer, dev_count))

    barrier = pltpu.get_barrier_semaphore()

    def greet(step, carry):
        pl.semaphore_signal(barrier, inc=1, device_id=peer_id(step)[1], device_id_type=MESH)
        return carry

    lax.fori_loop(1, total, greet, 0)
    pl.semaphore_wait(barrier, total - 1)

    def send(step, carry):
        peer, device = peer_id(step)
        for index in range(count):
            pltpu.make_async_remote_copy(
                src_ref=sources[index].at[pl.ds(peer, 1)],
                dst_ref=landings[index].at[pl.ds(me, 1)],
                send_sem=send_sems.at[index],
                recv_sem=recv_sems.at[index],
                device_id=device,
                device_id_type=MESH,
            ).start()
        return carry

    lax.fori_loop(1, total, send, 0)
    for index in range(count):
        landings[index][pl.ds(me, 1)] = sources[index][pl.ds(me, 1)]
    for index in range(count):
        every = pltpu.make_async_remote_copy(
            src_ref=sources[index].at[pl.ds(0, total - 1)],
            dst_ref=landings[index].at[pl.ds(0, total - 1)],
            send_sem=send_sems.at[index],
            recv_sem=recv_sems.at[index],
            device_id=peer_id(1)[1],
            device_id_type=MESH,
        )
        every.wait_send()
        every.wait_recv()
    for index in range(count):
        targets[index][...] = landings[index][...]


def exchange(arrays, dev_count, tag):
    count = len(arrays)
    return pl.pallas_call(
        functools.partial(exchange_kernel, dev_count, count),
        out_shape=[jax.ShapeDtypeStruct(array.shape, array.dtype) for array in arrays],
        in_specs=[pl.BlockSpec(memory_space=pltpu.VMEM)] * count,
        out_specs=[pl.BlockSpec(memory_space=pltpu.VMEM)] * count,
        scratch_shapes=[pltpu.VMEM(array.shape, array.dtype) for array in arrays]
        + [pltpu.SemaphoreType.DMA((count,)), pltpu.SemaphoreType.DMA((count,))],
        compiler_params=pltpu.CompilerParams(collective_id=tag, has_side_effects=True),
    )(*arrays)


def widen(small, feat_width):
    return jnp.pad(small.astype(jnp.float32), ((0, 0), (0, feat_width - small.shape[1])))


def local(queries, passages, candidates, location):
    group_count = lax.axis_size("group")
    dev_count = lax.axis_size("dev")
    device_total = group_count * dev_count
    query_count, query_len, feat_width = queries.shape
    pass_count = passages.shape[0]
    list_len = candidates.shape[1]
    pair_count = query_count * list_len
    slot_cap = max(2, (3 * pair_count + device_total - 1) // device_total)
    slot_total = device_total * slot_cap
    query_unit, query_scale = normalize(queries)
    query_send = query_unit.astype(jnp.bfloat16)
    passage_unit = normalize(passages)[0].astype(jnp.bfloat16)
    rows = jnp.take(location, candidates.reshape(-1), axis=0)
    target = rows // pass_count
    local_row = rows % pass_count
    same_target = target[:, None] == target[None, :]
    positions = jnp.arange(pair_count, dtype=jnp.int32)
    earlier = positions[None, :] < positions[:, None]
    before = jnp.sum(same_target & earlier, axis=1)
    slot_index = target * slot_cap + before
    pair_of_slot = jnp.zeros((slot_total,), jnp.int32).at[slot_index].set(positions)
    outgoing = jnp.take(query_send, pair_of_slot // list_len, axis=0)
    labels = jnp.take(local_row, pair_of_slot, axis=0).astype(jnp.bfloat16)
    both_axes = ("group", "dev")
    outgoing = outgoing.reshape(device_total, slot_cap, query_len, feat_width)
    labels = labels.reshape(device_total, slot_cap)
    first_arrived, tags = exchange([outgoing[:, 0], widen(labels, feat_width)], dev_count, 0)
    tags = tags[:, :slot_cap].astype(jnp.int32)
    block_rows = 64

    def score_block(inputs):
        query_block, tag_block = inputs
        passage_block = jnp.take(passage_unit, tag_block, axis=0)
        logits = (
            jnp.einsum(
                "bqe,bpe->bqp", query_block, passage_block, preferred_element_type=jnp.float32
            )
            / SOFTNESS
        )
        exp_terms = jnp.exp(logits)
        token_mass = jnp.sum(exp_terms, axis=-1, keepdims=True)
        pair_score = jnp.sum(SOFTNESS * jnp.log(token_mass[..., 0]), axis=-1)
        attention = (exp_terms / token_mass).astype(jnp.bfloat16)
        pulled = jnp.einsum(
            "bqp,bpe->bqe", attention, passage_block, preferred_element_type=jnp.float32
        )
        return (pulled.astype(jnp.bfloat16), pair_score)

    returned = []
    scores = []
    for slot in range(slot_cap):
        if slot == 0:
            arrived = first_arrived
        else:
            arrived = lax.all_to_all(
                outgoing[:, slot], both_axes, split_axis=0, concat_axis=0, tiled=True
            )
        blocks = device_total // block_rows
        pulled, score = lax.map(
            score_block,
            (
                arrived.reshape(blocks, block_rows, query_len, feat_width),
                tags[:, slot].reshape(blocks, block_rows),
            ),
        )
        pulled = pulled.reshape(device_total, query_len, feat_width)
        scores.append(score.reshape(device_total))
        if slot < slot_cap - 1:
            returned.append(
                lax.all_to_all(pulled, both_axes, split_axis=0, concat_axis=0, tiled=True)
            )
    scores = jnp.stack(scores, axis=1)
    last_returned, scores_flat = exchange([pulled, widen(scores, feat_width)], dev_count, 1)
    returned.append(last_returned)
    scores_flat = scores_flat[:, :slot_cap]
    pair_score = jnp.take(scores_flat.reshape(slot_total), slot_index, axis=0).reshape(
        query_count, list_len
    )
    pair_pulled = jnp.take(returned[0], target, axis=0)
    for slot in range(1, slot_cap):
        pair_pulled = jnp.where(
            (before == slot)[:, None, None], jnp.take(returned[slot], target, axis=0), pair_pulled
        )
    pair_pulled = pair_pulled.reshape(query_count, list_len, query_len, feat_width)
    exp_scores = jnp.exp(pair_score)
    total = jnp.sum(exp_scores, axis=-1, keepdims=True)
    loss = jnp.log(total[:, 0]) - pair_score[:, 0]
    first = (jnp.arange(list_len) == 0).astype(jnp.float32)
    coeff = exp_scores / total - first[None, :]
    unit_grad = jnp.einsum("bk,bkqe->bqe", coeff, pair_pulled.astype(jnp.float32))
    along = jnp.sum(query_unit * unit_grad, axis=-1, keepdims=True)
    query_grad = (unit_grad - query_unit * along) * query_scale
    return (loss, query_grad)


def solution(mesh):
    placed = (
        P(("group", "dev"), None, None),
        P(("group", "dev"), None, None),
        P(("group", "dev"), None),
        P(),
    )
    return jax.shard_map(
        local,
        mesh=mesh,
        in_specs=placed,
        out_specs=(P(("group", "dev")), P(("group", "dev"), None, None)),
        check_vma=False,
    )
```

```python
import functools

import jax
import jax.numpy as jnp
from jax import lax
from jax.experimental import pallas as pl
from jax.experimental.pallas import tpu as pltpu
from jax.sharding import PartitionSpec as P

MESH = pl.DeviceIdType.MESH

SOFTNESS = 0.02
EPSILON = 1e-06


def normalize(values):
    floats = values.astype(jnp.float32)
    scale = lax.rsqrt(jnp.sum(floats * floats, axis=-1, keepdims=True) + EPSILON)
    return (floats * scale, scale)


def exchange_kernel(dev_count, count, *refs):
    sources, targets = refs[:count], refs[count : 2 * count]
    landings = refs[2 * count : 3 * count]
    send_sems, recv_sems = refs[3 * count], refs[3 * count + 1]
    total = sources[0].shape[0]
    me = lax.axis_index("group") * dev_count + lax.axis_index("dev")

    def peer_id(step):
        peer = lax.rem(me + step, total)
        return peer, (lax.div(peer, dev_count), lax.rem(peer, dev_count))

    barrier = pltpu.get_barrier_semaphore()

    def greet(step, carry):
        pl.semaphore_signal(barrier, inc=1, device_id=peer_id(step)[1], device_id_type=MESH)
        return carry

    lax.fori_loop(1, total, greet, 0)
    pl.semaphore_wait(barrier, total - 1)

    def send(step, carry):
        peer, device = peer_id(step)
        for index in range(count):
            pltpu.make_async_remote_copy(
                src_ref=sources[index].at[pl.ds(peer, 1)],
                dst_ref=landings[index].at[pl.ds(me, 1)],
                send_sem=send_sems.at[index],
                recv_sem=recv_sems.at[index],
                device_id=device,
                device_id_type=MESH,
            ).start()
        return carry

    lax.fori_loop(1, total, send, 0)
    for index in range(count):
        landings[index][pl.ds(me, 1)] = sources[index][pl.ds(me, 1)]
    for index in range(count):
        every = pltpu.make_async_remote_copy(
            src_ref=sources[index].at[pl.ds(0, total - 1)],
            dst_ref=landings[index].at[pl.ds(0, total - 1)],
            send_sem=send_sems.at[index],
            recv_sem=recv_sems.at[index],
            device_id=peer_id(1)[1],
            device_id_type=MESH,
        )
        every.wait_send()
        every.wait_recv()
    for index in range(count):
        targets[index][...] = landings[index][...]


def exchange(arrays, dev_count, tag):
    count = len(arrays)
    return pl.pallas_call(
        functools.partial(exchange_kernel, dev_count, count),
        out_shape=[jax.ShapeDtypeStruct(array.shape, array.dtype) for array in arrays],
        in_specs=[pl.BlockSpec(memory_space=pltpu.VMEM)] * count,
        out_specs=[pl.BlockSpec(memory_space=pltpu.VMEM)] * count,
        scratch_shapes=[pltpu.VMEM(array.shape, array.dtype) for array in arrays]
        + [pltpu.SemaphoreType.DMA((count,)), pltpu.SemaphoreType.DMA((count,))],
        compiler_params=pltpu.CompilerParams(collective_id=tag, has_side_effects=True),
    )(*arrays)


def widen(small, feat_width):
    return jnp.pad(small.astype(jnp.float32), ((0, 0), (0, feat_width - small.shape[1])))


def local(queries, passages, candidates, location):
    group_count = lax.axis_size("group")
    dev_count = lax.axis_size("dev")
    device_total = group_count * dev_count
    query_count, query_len, feat_width = queries.shape
    pass_count = passages.shape[0]
    list_len = candidates.shape[1]
    pair_count = query_count * list_len
    slot_cap = max(2, (3 * pair_count + device_total - 1) // device_total)
    slot_total = device_total * slot_cap
    query_unit, query_scale = normalize(queries)
    query_send = query_unit.astype(jnp.bfloat16)
    passage_unit = normalize(passages)[0].astype(jnp.bfloat16)
    rows = jnp.take(location, candidates.reshape(-1), axis=0)
    target = rows // pass_count
    local_row = rows % pass_count
    same_target = target[:, None] == target[None, :]
    positions = jnp.arange(pair_count, dtype=jnp.int32)
    earlier = positions[None, :] < positions[:, None]
    before = jnp.sum(same_target & earlier, axis=1)
    slot_index = target * slot_cap + before
    pair_of_slot = jnp.zeros((slot_total,), jnp.int32).at[slot_index].set(positions)
    outgoing = jnp.take(query_send, pair_of_slot // list_len, axis=0)
    labels = jnp.take(local_row, pair_of_slot, axis=0).astype(jnp.bfloat16)
    both_axes = ("group", "dev")
    outgoing = outgoing.reshape(device_total, slot_cap, query_len, feat_width)
    labels = labels.reshape(device_total, slot_cap)
    first_arrived, tags = exchange([outgoing[:, 0], widen(labels, feat_width)], dev_count, 0)
    first_arrived, tags, outgoing = lax.optimization_barrier((first_arrived, tags, outgoing))
    tags = tags[:, :slot_cap].astype(jnp.int32)
    block_rows = 64

    def score_block(inputs):
        query_block, tag_block = inputs
        passage_block = jnp.take(passage_unit, tag_block, axis=0)
        logits = (
            jnp.einsum(
                "bqe,bpe->bqp", query_block, passage_block, preferred_element_type=jnp.float32
            )
            / SOFTNESS
        )
        exp_terms = jnp.exp(logits)
        token_mass = jnp.sum(exp_terms, axis=-1, keepdims=True)
        pair_score = jnp.sum(SOFTNESS * jnp.log(token_mass[..., 0]), axis=-1)
        attention = (exp_terms / token_mass).astype(jnp.bfloat16)
        pulled = jnp.einsum(
            "bqp,bpe->bqe", attention, passage_block, preferred_element_type=jnp.float32
        )
        return (pulled.astype(jnp.bfloat16), pair_score)

    returned = []
    scores = []
    for slot in range(slot_cap):
        if slot == 0:
            arrived = first_arrived
        else:
            arrived = lax.all_to_all(
                outgoing[:, slot], both_axes, split_axis=0, concat_axis=0, tiled=True
            )
        blocks = device_total // block_rows
        pulled, score = lax.map(
            score_block,
            (
                arrived.reshape(blocks, block_rows, query_len, feat_width),
                tags[:, slot].reshape(blocks, block_rows),
            ),
        )
        pulled = pulled.reshape(device_total, query_len, feat_width)
        scores.append(score.reshape(device_total))
        if slot < slot_cap - 1:
            returned.append(
                lax.all_to_all(pulled, both_axes, split_axis=0, concat_axis=0, tiled=True)
            )
    scores = jnp.stack(scores, axis=1)
    pulled, scores, returned[0] = lax.optimization_barrier((pulled, scores, returned[0]))
    last_returned, scores_flat = exchange([pulled, widen(scores, feat_width)], dev_count, 1)
    returned.append(last_returned)
    scores_flat = scores_flat[:, :slot_cap]
    pair_score = jnp.take(scores_flat.reshape(slot_total), slot_index, axis=0).reshape(
        query_count, list_len
    )
    pair_pulled = jnp.take(returned[0], target, axis=0)
    for slot in range(1, slot_cap):
        pair_pulled = jnp.where(
            (before == slot)[:, None, None], jnp.take(returned[slot], target, axis=0), pair_pulled
        )
    pair_pulled = pair_pulled.reshape(query_count, list_len, query_len, feat_width)
    exp_scores = jnp.exp(pair_score)
    total = jnp.sum(exp_scores, axis=-1, keepdims=True)
    loss = jnp.log(total[:, 0]) - pair_score[:, 0]
    first = (jnp.arange(list_len) == 0).astype(jnp.float32)
    coeff = exp_scores / total - first[None, :]
    unit_grad = jnp.einsum("bk,bkqe->bqe", coeff, pair_pulled.astype(jnp.float32))
    along = jnp.sum(query_unit * unit_grad, axis=-1, keepdims=True)
    query_grad = (unit_grad - query_unit * along) * query_scale
    return (loss, query_grad)


def solution(mesh):
    placed = (
        P(("group", "dev"), None, None),
        P(("group", "dev"), None, None),
        P(("group", "dev"), None),
        P(),
    )
    return jax.shard_map(
        local,
        mesh=mesh,
        in_specs=placed,
        out_specs=(P(("group", "dev")), P(("group", "dev"), None, None)),
        check_vma=False,
    )
```

```python
import functools

import jax
import jax.numpy as jnp
from jax import lax
from jax.experimental import pallas as pl
from jax.experimental.pallas import tpu as pltpu
from jax.sharding import PartitionSpec as P

MESH = pl.DeviceIdType.MESH

SOFTNESS = 0.02
EPSILON = 1e-06


def normalize(values):
    floats = values.astype(jnp.float32)
    scale = lax.rsqrt(jnp.sum(floats * floats, axis=-1, keepdims=True) + EPSILON)
    return (floats * scale, scale)


def exchange_kernel(dev_count, count, *refs):
    sources, targets = refs[:count], refs[count : 2 * count]
    landings = refs[2 * count : 3 * count]
    send_sems, recv_sems = refs[3 * count], refs[3 * count + 1]
    total = sources[0].shape[0]
    me = lax.axis_index("group") * dev_count + lax.axis_index("dev")

    def peer_id(step):
        reach = lax.div(step + 1, 2)
        offset = jnp.where(lax.rem(step, 2) == 1, reach, total - reach)
        peer = lax.rem(me + offset, total)
        return peer, (lax.div(peer, dev_count), lax.rem(peer, dev_count))

    barrier = pltpu.get_barrier_semaphore()

    def greet(step, carry):
        pl.semaphore_signal(barrier, inc=1, device_id=peer_id(step)[1], device_id_type=MESH)
        return carry

    lax.fori_loop(1, total, greet, 0)
    pl.semaphore_wait(barrier, total - 1)

    def send(step, carry):
        peer, device = peer_id(step)
        for index in range(count):
            pltpu.make_async_remote_copy(
                src_ref=sources[index].at[pl.ds(peer, 1)],
                dst_ref=landings[index].at[pl.ds(me, 1)],
                send_sem=send_sems.at[index],
                recv_sem=recv_sems.at[index],
                device_id=device,
                device_id_type=MESH,
            ).start()
        return carry

    lax.fori_loop(1, total, send, 0)
    for index in range(count):
        landings[index][pl.ds(me, 1)] = sources[index][pl.ds(me, 1)]
    for index in range(count):
        every = pltpu.make_async_remote_copy(
            src_ref=sources[index].at[pl.ds(0, total - 1)],
            dst_ref=landings[index].at[pl.ds(0, total - 1)],
            send_sem=send_sems.at[index],
            recv_sem=recv_sems.at[index],
            device_id=peer_id(1)[1],
            device_id_type=MESH,
        )
        every.wait_send()
        every.wait_recv()
    for index in range(count):
        targets[index][...] = landings[index][...]


def exchange(arrays, dev_count, tag):
    count = len(arrays)
    return pl.pallas_call(
        functools.partial(exchange_kernel, dev_count, count),
        out_shape=[jax.ShapeDtypeStruct(array.shape, array.dtype) for array in arrays],
        in_specs=[pl.BlockSpec(memory_space=pltpu.VMEM)] * count,
        out_specs=[pl.BlockSpec(memory_space=pltpu.VMEM)] * count,
        scratch_shapes=[pltpu.VMEM(array.shape, array.dtype) for array in arrays]
        + [pltpu.SemaphoreType.DMA((count,)), pltpu.SemaphoreType.DMA((count,))],
        compiler_params=pltpu.CompilerParams(collective_id=tag, has_side_effects=True),
    )(*arrays)


def widen(small, feat_width):
    return jnp.pad(small.astype(jnp.float32), ((0, 0), (0, feat_width - small.shape[1])))


def local(queries, passages, candidates, location):
    group_count = lax.axis_size("group")
    dev_count = lax.axis_size("dev")
    device_total = group_count * dev_count
    query_count, query_len, feat_width = queries.shape
    pass_count = passages.shape[0]
    list_len = candidates.shape[1]
    pair_count = query_count * list_len
    slot_cap = max(2, (3 * pair_count + device_total - 1) // device_total)
    slot_total = device_total * slot_cap
    query_unit, query_scale = normalize(queries)
    query_send = query_unit.astype(jnp.bfloat16)
    passage_unit = normalize(passages)[0].astype(jnp.bfloat16)
    rows = jnp.take(location, candidates.reshape(-1), axis=0)
    target = rows // pass_count
    local_row = rows % pass_count
    same_target = target[:, None] == target[None, :]
    positions = jnp.arange(pair_count, dtype=jnp.int32)
    earlier = positions[None, :] < positions[:, None]
    before = jnp.sum(same_target & earlier, axis=1)
    slot_index = target * slot_cap + before
    pair_of_slot = jnp.zeros((slot_total,), jnp.int32).at[slot_index].set(positions)
    outgoing = jnp.take(query_send, pair_of_slot // list_len, axis=0)
    labels = jnp.take(local_row, pair_of_slot, axis=0).astype(jnp.bfloat16)
    both_axes = ("group", "dev")
    outgoing = outgoing.reshape(device_total, slot_cap, query_len, feat_width)
    labels = labels.reshape(device_total, slot_cap)
    first_arrived, tags = exchange([outgoing[:, 0], widen(labels, feat_width)], dev_count, 0)
    first_arrived, tags, outgoing = lax.optimization_barrier((first_arrived, tags, outgoing))
    tags = tags[:, :slot_cap].astype(jnp.int32)
    block_rows = 64

    def score_block(inputs):
        query_block, tag_block = inputs
        passage_block = jnp.take(passage_unit, tag_block, axis=0)
        logits = (
            jnp.einsum(
                "bqe,bpe->bqp", query_block, passage_block, preferred_element_type=jnp.float32
            )
            / SOFTNESS
        )
        exp_terms = jnp.exp(logits)
        token_mass = jnp.sum(exp_terms, axis=-1, keepdims=True)
        pair_score = jnp.sum(SOFTNESS * jnp.log(token_mass[..., 0]), axis=-1)
        attention = (exp_terms / token_mass).astype(jnp.bfloat16)
        pulled = jnp.einsum(
            "bqp,bpe->bqe", attention, passage_block, preferred_element_type=jnp.float32
        )
        return (pulled.astype(jnp.bfloat16), pair_score)

    returned = []
    scores = []
    for slot in range(slot_cap):
        if slot == 0:
            arrived = first_arrived
        else:
            arrived = lax.all_to_all(
                outgoing[:, slot], both_axes, split_axis=0, concat_axis=0, tiled=True
            )
        blocks = device_total // block_rows
        pulled, score = lax.map(
            score_block,
            (
                arrived.reshape(blocks, block_rows, query_len, feat_width),
                tags[:, slot].reshape(blocks, block_rows),
            ),
        )
        pulled = pulled.reshape(device_total, query_len, feat_width)
        scores.append(score.reshape(device_total))
        if slot < slot_cap - 1:
            returned.append(
                lax.all_to_all(pulled, both_axes, split_axis=0, concat_axis=0, tiled=True)
            )
    scores = jnp.stack(scores, axis=1)
    pulled, scores, returned[0] = lax.optimization_barrier((pulled, scores, returned[0]))
    last_returned, scores_flat = exchange([pulled, widen(scores, feat_width)], dev_count, 1)
    returned.append(last_returned)
    scores_flat = scores_flat[:, :slot_cap]
    pair_score = jnp.take(scores_flat.reshape(slot_total), slot_index, axis=0).reshape(
        query_count, list_len
    )
    pair_pulled = jnp.take(returned[0], target, axis=0)
    for slot in range(1, slot_cap):
        pair_pulled = jnp.where(
            (before == slot)[:, None, None], jnp.take(returned[slot], target, axis=0), pair_pulled
        )
    pair_pulled = pair_pulled.reshape(query_count, list_len, query_len, feat_width)
    exp_scores = jnp.exp(pair_score)
    total = jnp.sum(exp_scores, axis=-1, keepdims=True)
    loss = jnp.log(total[:, 0]) - pair_score[:, 0]
    first = (jnp.arange(list_len) == 0).astype(jnp.float32)
    coeff = exp_scores / total - first[None, :]
    unit_grad = jnp.einsum("bk,bkqe->bqe", coeff, pair_pulled.astype(jnp.float32))
    along = jnp.sum(query_unit * unit_grad, axis=-1, keepdims=True)
    query_grad = (unit_grad - query_unit * along) * query_scale
    return (loss, query_grad)


def solution(mesh):
    placed = (
        P(("group", "dev"), None, None),
        P(("group", "dev"), None, None),
        P(("group", "dev"), None),
        P(),
    )
    return jax.shard_map(
        local,
        mesh=mesh,
        in_specs=placed,
        out_specs=(P(("group", "dev")), P(("group", "dev"), None, None)),
        check_vma=False,
    )
```

```python
import functools

import jax
import jax.numpy as jnp
from jax import lax
from jax.experimental import pallas as pl
from jax.experimental.pallas import tpu as pltpu
from jax.sharding import PartitionSpec as P

MESH = pl.DeviceIdType.MESH

SOFTNESS = 0.02
EPSILON = 1e-06


def normalize(values):
    floats = values.astype(jnp.float32)
    scale = lax.rsqrt(jnp.sum(floats * floats, axis=-1, keepdims=True) + EPSILON)
    return (floats * scale, scale)


def exchange_kernel(dev_count, rows_ref, out_ref, landing, send_sem, recv_sem):
    total = rows_ref.shape[0]
    me = lax.axis_index("group") * dev_count + lax.axis_index("dev")

    def peer_id(step):
        peer = lax.rem(me + step, total)
        return peer, (lax.div(peer, dev_count), lax.rem(peer, dev_count))

    barrier = pltpu.get_barrier_semaphore()

    def greet(step, carry):
        pl.semaphore_signal(barrier, inc=1, device_id=peer_id(step)[1], device_id_type=MESH)
        return carry

    lax.fori_loop(1, total, greet, 0)
    pl.semaphore_wait(barrier, total - 1)

    def send(step, carry):
        peer, device = peer_id(step)
        pltpu.make_async_remote_copy(
            src_ref=rows_ref.at[pl.ds(peer, 1)],
            dst_ref=landing.at[pl.ds(me, 1)],
            send_sem=send_sem,
            recv_sem=recv_sem,
            device_id=device,
            device_id_type=MESH,
        ).start()
        return carry

    lax.fori_loop(1, total, send, 0)
    landing[pl.ds(me, 1), :] = rows_ref[pl.ds(me, 1), :]
    every = pltpu.make_async_remote_copy(
        src_ref=rows_ref.at[pl.ds(0, total - 1)],
        dst_ref=landing.at[pl.ds(0, total - 1)],
        send_sem=send_sem,
        recv_sem=recv_sem,
        device_id=peer_id(1)[1],
        device_id_type=MESH,
    )
    every.wait_send()
    every.wait_recv()
    out_ref[...] = landing[...]


def exchange(rows, dev_count, tag):
    return pl.pallas_call(
        functools.partial(exchange_kernel, dev_count),
        out_shape=jax.ShapeDtypeStruct(rows.shape, rows.dtype),
        in_specs=[pl.BlockSpec(memory_space=pltpu.VMEM)],
        out_specs=pl.BlockSpec(memory_space=pltpu.VMEM),
        scratch_shapes=[
            pltpu.VMEM(rows.shape, rows.dtype),
            pltpu.SemaphoreType.DMA(()),
            pltpu.SemaphoreType.DMA(()),
        ],
        compiler_params=pltpu.CompilerParams(collective_id=tag, has_side_effects=True),
    )(rows)


def widen(small, feat_width):
    return jnp.pad(small.astype(jnp.float32), ((0, 0), (0, feat_width - small.shape[1])))


def local(queries, passages, candidates, location):
    group_count = lax.axis_size("group")
    dev_count = lax.axis_size("dev")
    device_total = group_count * dev_count
    query_count, query_len, feat_width = queries.shape
    pass_count = passages.shape[0]
    list_len = candidates.shape[1]
    pair_count = query_count * list_len
    slot_cap = max(2, (3 * pair_count + device_total - 1) // device_total)
    slot_total = device_total * slot_cap
    query_unit, query_scale = normalize(queries)
    query_send = query_unit.astype(jnp.bfloat16)
    passage_unit = normalize(passages)[0].astype(jnp.bfloat16)
    rows = jnp.take(location, candidates.reshape(-1), axis=0)
    target = rows // pass_count
    local_row = rows % pass_count
    same_target = target[:, None] == target[None, :]
    positions = jnp.arange(pair_count, dtype=jnp.int32)
    earlier = positions[None, :] < positions[:, None]
    before = jnp.sum(same_target & earlier, axis=1)
    slot_index = target * slot_cap + before
    pair_of_slot = jnp.zeros((slot_total,), jnp.int32).at[slot_index].set(positions)
    slot_owner = (pair_of_slot // list_len).reshape(device_total, slot_cap)
    labels = jnp.take(local_row, pair_of_slot, axis=0, mode="clip").astype(jnp.bfloat16)
    both_axes = ("group", "dev")
    labels = labels.reshape(device_total, slot_cap)
    tags = exchange(widen(labels, feat_width), dev_count, 0)[:, :slot_cap].astype(jnp.int32)
    block_rows = 64

    def score_block(inputs):
        query_block, tag_block = inputs
        passage_block = jnp.take(passage_unit, tag_block, axis=0, mode="clip")
        logits = (
            jnp.einsum(
                "bqe,bpe->bqp", query_block, passage_block, preferred_element_type=jnp.float32
            )
            / SOFTNESS
        )
        exp_terms = jnp.exp(logits)
        token_mass = jnp.sum(exp_terms, axis=-1, keepdims=True)
        pair_score = jnp.sum(SOFTNESS * jnp.log(token_mass[..., 0]), axis=-1)
        attention = (exp_terms / token_mass).astype(jnp.bfloat16)
        pulled = jnp.einsum(
            "bqp,bpe->bqe", attention, passage_block, preferred_element_type=jnp.float32
        )
        return (pulled.astype(jnp.bfloat16), pair_score)

    returned = []
    scores = []
    for slot in range(slot_cap):
        outgoing = jnp.take(query_send, slot_owner[:, slot], axis=0, mode="clip")
        arrived = lax.all_to_all(outgoing, both_axes, split_axis=0, concat_axis=0, tiled=True)
        blocks = device_total // block_rows
        pulled, score = lax.map(
            score_block,
            (
                arrived.reshape(blocks, block_rows, query_len, feat_width),
                tags[:, slot].reshape(blocks, block_rows),
            ),
        )
        pulled = pulled.reshape(device_total, query_len, feat_width)
        returned.append(lax.all_to_all(pulled, both_axes, split_axis=0, concat_axis=0, tiled=True))
        scores.append(score.reshape(device_total))
    scores = jnp.stack(scores, axis=1)
    scores, returned[-1] = lax.optimization_barrier((scores, returned[-1]))
    scores_flat = exchange(widen(scores, feat_width), dev_count, 1)[:, :slot_cap]
    pair_score = jnp.take(scores_flat.reshape(slot_total), slot_index, axis=0, mode="clip").reshape(
        query_count, list_len
    )
    pair_pulled = jnp.take(returned[0], target, axis=0, mode="clip")
    for slot in range(1, slot_cap):
        pair_pulled = jnp.where(
            (before == slot)[:, None, None], jnp.take(returned[slot], target, axis=0, mode="clip"), pair_pulled
        )
    pair_pulled = pair_pulled.reshape(query_count, list_len, query_len, feat_width)
    exp_scores = jnp.exp(pair_score)
    total = jnp.sum(exp_scores, axis=-1, keepdims=True)
    loss = jnp.log(total[:, 0]) - pair_score[:, 0]
    first = (jnp.arange(list_len) == 0).astype(jnp.float32)
    coeff = exp_scores / total - first[None, :]
    unit_grad = jnp.einsum("bk,bkqe->bqe", coeff, pair_pulled.astype(jnp.float32))
    along = jnp.sum(query_unit * unit_grad, axis=-1, keepdims=True)
    query_grad = (unit_grad - query_unit * along) * query_scale
    return (loss, query_grad)


def solution(mesh):
    placed = (
        P(("group", "dev"), None, None),
        P(("group", "dev"), None, None),
        P(("group", "dev"), None),
        P(),
    )
    return jax.shard_map(
        local,
        mesh=mesh,
        in_specs=placed,
        out_specs=(P(("group", "dev")), P(("group", "dev"), None, None)),
        check_vma=False,
    )
```

```python
import functools

import jax
import jax.numpy as jnp
from jax import lax
from jax.experimental import pallas as pl
from jax.experimental.pallas import tpu as pltpu
from jax.sharding import PartitionSpec as P

MESH = pl.DeviceIdType.MESH

SOFTNESS = 0.02
EPSILON = 1e-06


def normalize(values):
    floats = values.astype(jnp.float32)
    scale = lax.rsqrt(jnp.sum(floats * floats, axis=-1, keepdims=True) + EPSILON)
    return (floats * scale, scale)


def exchange_kernel(dev_count, rows_ref, out_ref, landing, send_sem, recv_sem):
    total = rows_ref.shape[0]
    me = lax.axis_index("group") * dev_count + lax.axis_index("dev")

    def peer_id(step):
        peer = lax.rem(me + step, total)
        return peer, (lax.div(peer, dev_count), lax.rem(peer, dev_count))

    barrier = pltpu.get_barrier_semaphore()

    def greet(step, carry):
        pl.semaphore_signal(barrier, inc=1, device_id=peer_id(step)[1], device_id_type=MESH)
        return carry

    lax.fori_loop(1, total, greet, 0)
    pl.semaphore_wait(barrier, total - 1)

    def send(step, carry):
        peer, device = peer_id(step)
        pltpu.make_async_remote_copy(
            src_ref=rows_ref.at[pl.ds(peer, 1)],
            dst_ref=landing.at[pl.ds(me, 1)],
            send_sem=send_sem,
            recv_sem=recv_sem,
            device_id=device,
            device_id_type=MESH,
        ).start()
        return carry

    lax.fori_loop(1, total, send, 0)
    landing[pl.ds(me, 1), :] = rows_ref[pl.ds(me, 1), :]
    every = pltpu.make_async_remote_copy(
        src_ref=rows_ref.at[pl.ds(0, total - 1)],
        dst_ref=landing.at[pl.ds(0, total - 1)],
        send_sem=send_sem,
        recv_sem=recv_sem,
        device_id=peer_id(1)[1],
        device_id_type=MESH,
    )
    every.wait_send()
    every.wait_recv()
    out_ref[...] = landing[...]


def exchange(rows, dev_count, tag):
    return pl.pallas_call(
        functools.partial(exchange_kernel, dev_count),
        out_shape=jax.ShapeDtypeStruct(rows.shape, rows.dtype),
        in_specs=[pl.BlockSpec(memory_space=pltpu.VMEM)],
        out_specs=pl.BlockSpec(memory_space=pltpu.VMEM),
        scratch_shapes=[
            pltpu.VMEM(rows.shape, rows.dtype),
            pltpu.SemaphoreType.DMA(()),
            pltpu.SemaphoreType.DMA(()),
        ],
        compiler_params=pltpu.CompilerParams(collective_id=tag, has_side_effects=True),
    )(rows)


def widen(small, feat_width):
    return jnp.pad(small.astype(jnp.float32), ((0, 0), (0, feat_width - small.shape[1])))


def local(queries, passages, candidates, location):
    group_count = lax.axis_size("group")
    dev_count = lax.axis_size("dev")
    device_total = group_count * dev_count
    query_count, query_len, feat_width = queries.shape
    pass_count = passages.shape[0]
    list_len = candidates.shape[1]
    pair_count = query_count * list_len
    slot_cap = max(2, (3 * pair_count + device_total - 1) // device_total)
    slot_total = device_total * slot_cap
    query_unit, query_scale = normalize(queries)
    query_send = query_unit.astype(jnp.bfloat16)
    passage_unit = normalize(passages)[0].astype(jnp.bfloat16)
    rows = jnp.take(location, candidates.reshape(-1), axis=0)
    target = rows // pass_count
    local_row = rows % pass_count
    same_target = target[:, None] == target[None, :]
    positions = jnp.arange(pair_count, dtype=jnp.int32)
    earlier = positions[None, :] < positions[:, None]
    before = jnp.sum(same_target & earlier, axis=1)
    slot_index = target * slot_cap + before
    pair_of_slot = jnp.zeros((slot_total,), jnp.int32).at[slot_index].set(positions)
    slot_owner = (pair_of_slot // list_len).reshape(device_total, slot_cap)
    labels = jnp.take(local_row, pair_of_slot, axis=0, mode="clip").astype(jnp.bfloat16)
    both_axes = ("group", "dev")
    labels = labels.reshape(device_total, slot_cap)
    tags = exchange(widen(labels, feat_width), dev_count, 0)[:, :slot_cap].astype(jnp.int32)
    block_rows = 64

    def score_block(inputs):
        query_block, tag_block = inputs
        passage_block = jnp.take(passage_unit, tag_block, axis=0, mode="clip")
        logits = (
            jnp.einsum(
                "bqe,bpe->bqp", query_block, passage_block, preferred_element_type=jnp.float32
            )
            / SOFTNESS
        )
        exp_terms = jnp.exp(logits)
        token_mass = jnp.sum(exp_terms, axis=-1, keepdims=True)
        pair_score = jnp.sum(SOFTNESS * jnp.log(token_mass[..., 0]), axis=-1)
        attention = (exp_terms / token_mass).astype(jnp.bfloat16)
        pulled = jnp.einsum(
            "bqp,bpe->bqe", attention, passage_block, preferred_element_type=jnp.float32
        )
        return (pulled.astype(jnp.bfloat16), pair_score)

    returned = []
    scores = []
    pulled_parts = []
    for slot in range(slot_cap):
        outgoing = jnp.take(query_send, slot_owner[:, slot], axis=0, mode="clip")
        arrived = lax.all_to_all(outgoing, both_axes, split_axis=0, concat_axis=0, tiled=True)
        blocks = device_total // block_rows
        pulled, score = lax.map(
            score_block,
            (
                arrived.reshape(blocks, block_rows, query_len, feat_width),
                tags[:, slot].reshape(blocks, block_rows),
            ),
        )
        pulled_parts.append(pulled.reshape(device_total, query_len, feat_width))
        scores.append(score.reshape(device_total))
        if slot < slot_cap - 1:
            returned.append(
                lax.all_to_all(
                    pulled_parts[-1], both_axes, split_axis=0, concat_axis=0, tiled=True
                )
            )
    returned.append(
        lax.all_to_all(pulled_parts[-1], both_axes, split_axis=0, concat_axis=0, tiled=True)
    )
    scores = jnp.stack(scores, axis=1)
    scores_flat = exchange(widen(scores, feat_width), dev_count, 1)[:, :slot_cap]
    pair_score = jnp.take(scores_flat.reshape(slot_total), slot_index, axis=0, mode="clip").reshape(
        query_count, list_len
    )
    exp_scores = jnp.exp(pair_score)
    total = jnp.sum(exp_scores, axis=-1, keepdims=True)
    loss = jnp.log(total[:, 0]) - pair_score[:, 0]
    first = (jnp.arange(list_len) == 0).astype(jnp.float32)
    coeff = exp_scores / total - first[None, :]
    slot_of_pair = before.reshape(query_count, list_len)
    unit_grad = None
    for slot in range(slot_cap):
        part = jnp.take(returned[slot], target, axis=0, mode="clip").reshape(
            query_count, list_len, query_len, feat_width
        )
        weight = jnp.where(slot_of_pair == slot, coeff, 0.0)
        term = jnp.einsum("bk,bkqe->bqe", weight, part.astype(jnp.float32))
        unit_grad = term if unit_grad is None else unit_grad + term
    along = jnp.sum(query_unit * unit_grad, axis=-1, keepdims=True)
    query_grad = (unit_grad - query_unit * along) * query_scale
    return (loss, query_grad)


def solution(mesh):
    placed = (
        P(("group", "dev"), None, None),
        P(("group", "dev"), None, None),
        P(("group", "dev"), None),
        P(),
    )
    return jax.shard_map(
        local,
        mesh=mesh,
        in_specs=placed,
        out_specs=(P(("group", "dev")), P(("group", "dev"), None, None)),
        check_vma=False,
    )
```

```python
import functools

import jax
import jax.numpy as jnp
from jax import lax
from jax.experimental import pallas as pl
from jax.experimental.pallas import tpu as pltpu
from jax.sharding import PartitionSpec as P

MESH = pl.DeviceIdType.MESH

SOFTNESS = 0.02
EPSILON = 1e-06


def normalize(values):
    floats = values.astype(jnp.float32)
    scale = lax.rsqrt(jnp.sum(floats * floats, axis=-1, keepdims=True) + EPSILON)
    return (floats * scale, scale)


def exchange_kernel(dev_count, rows_ref, out_ref, landing, send_sem, recv_sem):
    total = rows_ref.shape[0]
    me = lax.axis_index("group") * dev_count + lax.axis_index("dev")

    def peer_id(step):
        peer = lax.rem(me + step, total)
        return peer, (lax.div(peer, dev_count), lax.rem(peer, dev_count))

    barrier = pltpu.get_barrier_semaphore()

    def greet(step, carry):
        pl.semaphore_signal(barrier, inc=1, device_id=peer_id(step)[1], device_id_type=MESH)
        return carry

    lax.fori_loop(1, total, greet, 0)
    pl.semaphore_wait(barrier, total - 1)

    def send(step, carry):
        peer, device = peer_id(step)
        pltpu.make_async_remote_copy(
            src_ref=rows_ref.at[pl.ds(peer, 1)],
            dst_ref=landing.at[pl.ds(me, 1)],
            send_sem=send_sem,
            recv_sem=recv_sem,
            device_id=device,
            device_id_type=MESH,
        ).start()
        return carry

    lax.fori_loop(1, total, send, 0)
    landing[pl.ds(me, 1), :] = rows_ref[pl.ds(me, 1), :]
    every = pltpu.make_async_remote_copy(
        src_ref=rows_ref.at[pl.ds(0, total - 1)],
        dst_ref=landing.at[pl.ds(0, total - 1)],
        send_sem=send_sem,
        recv_sem=recv_sem,
        device_id=peer_id(1)[1],
        device_id_type=MESH,
    )
    every.wait_send()
    every.wait_recv()
    out_ref[...] = landing[...]


def exchange(rows, dev_count, tag):
    return pl.pallas_call(
        functools.partial(exchange_kernel, dev_count),
        out_shape=jax.ShapeDtypeStruct(rows.shape, rows.dtype),
        in_specs=[pl.BlockSpec(memory_space=pltpu.VMEM)],
        out_specs=pl.BlockSpec(memory_space=pltpu.VMEM),
        scratch_shapes=[
            pltpu.VMEM(rows.shape, rows.dtype),
            pltpu.SemaphoreType.DMA(()),
            pltpu.SemaphoreType.DMA(()),
        ],
        compiler_params=pltpu.CompilerParams(collective_id=tag, has_side_effects=True),
    )(rows)


def widen(small, feat_width):
    return jnp.pad(small.astype(jnp.float32), ((0, 0), (0, feat_width - small.shape[1])))


def local(queries, passages, candidates, location):
    group_count = lax.axis_size("group")
    dev_count = lax.axis_size("dev")
    device_total = group_count * dev_count
    query_count, query_len, feat_width = queries.shape
    pass_count = passages.shape[0]
    list_len = candidates.shape[1]
    pair_count = query_count * list_len
    slot_cap = max(2, (3 * pair_count + device_total - 1) // device_total)
    slot_total = device_total * slot_cap
    query_unit, query_scale = normalize(queries)
    query_send = query_unit.astype(jnp.bfloat16)
    passage_unit = normalize(passages)[0].astype(jnp.bfloat16)
    rows = jnp.take(location, candidates.reshape(-1), axis=0)
    target = rows // pass_count
    local_row = rows % pass_count
    same_target = target[:, None] == target[None, :]
    positions = jnp.arange(pair_count, dtype=jnp.int32)
    earlier = positions[None, :] < positions[:, None]
    before = jnp.sum(same_target & earlier, axis=1)
    slot_index = target * slot_cap + before
    pair_of_slot = jnp.zeros((slot_total,), jnp.int32).at[slot_index].set(positions)
    slot_owner = (pair_of_slot // list_len).reshape(device_total, slot_cap)
    labels = jnp.take(local_row, pair_of_slot, axis=0, mode="clip").astype(jnp.bfloat16)
    both_axes = ("group", "dev")
    labels = labels.reshape(device_total, slot_cap)
    tags = exchange(widen(labels, feat_width), dev_count, 0)[:, :slot_cap].astype(jnp.int32)
    block_rows = 64

    def score_block(inputs):
        query_block, tag_block = inputs
        passage_block = jnp.take(passage_unit, tag_block, axis=0, mode="clip")
        logits = (
            jnp.einsum(
                "bqe,bpe->bqp", query_block, passage_block, preferred_element_type=jnp.float32
            )
            / SOFTNESS
        )
        exp_terms = jnp.exp(logits)
        token_mass = jnp.sum(exp_terms, axis=-1, keepdims=True)
        pair_score = jnp.sum(SOFTNESS * jnp.log(token_mass[..., 0]), axis=-1)
        attention = (exp_terms / token_mass).astype(jnp.bfloat16)
        pulled = jnp.einsum(
            "bqp,bpe->bqe", attention, passage_block, preferred_element_type=jnp.float32
        )
        return (pulled.astype(jnp.bfloat16), pair_score)

    returned = []
    scores = []
    pulled_parts = []
    for slot in range(slot_cap):
        outgoing = jnp.take(query_send, slot_owner[:, slot], axis=0, mode="clip")
        arrived = lax.all_to_all(outgoing, both_axes, split_axis=0, concat_axis=0, tiled=True)
        blocks = device_total // block_rows
        pulled, score = lax.map(
            score_block,
            (
                arrived.reshape(blocks, block_rows, query_len, feat_width),
                tags[:, slot].reshape(blocks, block_rows),
            ),
        )
        pulled_parts.append(pulled.reshape(device_total, query_len, feat_width))
        scores.append(score.reshape(device_total))
        if slot < slot_cap - 1:
            returned.append(
                lax.all_to_all(
                    pulled_parts[-1], both_axes, split_axis=0, concat_axis=0, tiled=True
                )
            )
    returned.append(
        lax.all_to_all(pulled_parts[-1], both_axes, split_axis=0, concat_axis=0, tiled=True)
    )
    scores = jnp.stack(scores, axis=1)
    first_part = jnp.take(returned[0], target, axis=0, mode="clip")
    scores, first_part = lax.optimization_barrier((scores, first_part))
    scores_flat = exchange(widen(scores, feat_width), dev_count, 1)[:, :slot_cap]
    pair_score = jnp.take(scores_flat.reshape(slot_total), slot_index, axis=0, mode="clip").reshape(
        query_count, list_len
    )
    exp_scores = jnp.exp(pair_score)
    total = jnp.sum(exp_scores, axis=-1, keepdims=True)
    loss = jnp.log(total[:, 0]) - pair_score[:, 0]
    first = (jnp.arange(list_len) == 0).astype(jnp.float32)
    coeff = exp_scores / total - first[None, :]
    slot_of_pair = before.reshape(query_count, list_len)
    unit_grad = None
    for slot in range(slot_cap):
        if slot == 0:
            part = first_part
        else:
            part = jnp.take(returned[slot], target, axis=0, mode="clip")
        part = part.reshape(query_count, list_len, query_len, feat_width)
        weight = jnp.where(slot_of_pair == slot, coeff, 0.0)
        term = jnp.einsum("bk,bkqe->bqe", weight, part.astype(jnp.float32))
        unit_grad = term if unit_grad is None else unit_grad + term
    along = jnp.sum(query_unit * unit_grad, axis=-1, keepdims=True)
    query_grad = (unit_grad - query_unit * along) * query_scale
    return (loss, query_grad)


def solution(mesh):
    placed = (
        P(("group", "dev"), None, None),
        P(("group", "dev"), None, None),
        P(("group", "dev"), None),
        P(),
    )
    return jax.shard_map(
        local,
        mesh=mesh,
        in_specs=placed,
        out_specs=(P(("group", "dev")), P(("group", "dev"), None, None)),
        check_vma=False,
    )
```

```python
import functools

import jax
import jax.numpy as jnp
from jax import lax
from jax.experimental import pallas as pl
from jax.experimental.pallas import tpu as pltpu
from jax.sharding import PartitionSpec as P

MESH = pl.DeviceIdType.MESH

SOFTNESS = 0.02
EPSILON = 1e-06


def normalize(values):
    floats = values.astype(jnp.float32)
    scale = lax.rsqrt(jnp.sum(floats * floats, axis=-1, keepdims=True) + EPSILON)
    return (floats * scale, scale)


def exchange_kernel(dev_count, rows_ref, out_ref, landing, send_sem, recv_sem):
    total = rows_ref.shape[0]
    me = lax.axis_index("group") * dev_count + lax.axis_index("dev")

    def peer_id(step):
        peer = lax.rem(me + step, total)
        return peer, (lax.div(peer, dev_count), lax.rem(peer, dev_count))

    barrier = pltpu.get_barrier_semaphore()

    def greet(step, carry):
        pl.semaphore_signal(barrier, inc=1, device_id=peer_id(step)[1], device_id_type=MESH)
        return carry

    lax.fori_loop(1, total, greet, 0)
    pl.semaphore_wait(barrier, total - 1)

    def send(step, carry):
        peer, device = peer_id(step)
        pltpu.make_async_remote_copy(
            src_ref=rows_ref.at[pl.ds(peer, 1)],
            dst_ref=landing.at[pl.ds(me, 1)],
            send_sem=send_sem,
            recv_sem=recv_sem,
            device_id=device,
            device_id_type=MESH,
        ).start()
        return carry

    lax.fori_loop(1, total, send, 0)
    landing[pl.ds(me, 1), :] = rows_ref[pl.ds(me, 1), :]
    every = pltpu.make_async_remote_copy(
        src_ref=rows_ref.at[pl.ds(0, total - 1)],
        dst_ref=landing.at[pl.ds(0, total - 1)],
        send_sem=send_sem,
        recv_sem=recv_sem,
        device_id=peer_id(1)[1],
        device_id_type=MESH,
    )
    every.wait_send()
    every.wait_recv()
    out_ref[...] = landing[...]


def exchange(rows, dev_count, tag):
    return pl.pallas_call(
        functools.partial(exchange_kernel, dev_count),
        out_shape=jax.ShapeDtypeStruct(rows.shape, rows.dtype),
        in_specs=[pl.BlockSpec(memory_space=pltpu.VMEM)],
        out_specs=pl.BlockSpec(memory_space=pltpu.VMEM),
        scratch_shapes=[
            pltpu.VMEM(rows.shape, rows.dtype),
            pltpu.SemaphoreType.DMA(()),
            pltpu.SemaphoreType.DMA(()),
        ],
        compiler_params=pltpu.CompilerParams(collective_id=tag, has_side_effects=True),
    )(rows)


def widen(small, feat_width):
    return jnp.pad(small.astype(jnp.float32), ((0, 0), (0, feat_width - small.shape[1])))


def local(queries, passages, candidates, location):
    group_count = lax.axis_size("group")
    dev_count = lax.axis_size("dev")
    device_total = group_count * dev_count
    query_count, query_len, feat_width = queries.shape
    pass_count = passages.shape[0]
    list_len = candidates.shape[1]
    pair_count = query_count * list_len
    slot_cap = max(2, (3 * pair_count + device_total - 1) // device_total)
    slot_total = device_total * slot_cap
    query_unit, query_scale = normalize(queries)
    query_send = query_unit.astype(jnp.bfloat16)
    passage_unit = normalize(passages)[0].astype(jnp.bfloat16)
    rows = jnp.take(location, candidates.reshape(-1), axis=0)
    target = rows // pass_count
    local_row = rows % pass_count
    same_target = target[:, None] == target[None, :]
    positions = jnp.arange(pair_count, dtype=jnp.int32)
    earlier = positions[None, :] < positions[:, None]
    before = jnp.sum(same_target & earlier, axis=1)
    slot_index = target * slot_cap + before
    pair_of_slot = jnp.zeros((slot_total,), jnp.int32).at[slot_index].set(positions)
    slot_owner = (pair_of_slot // list_len).reshape(device_total, slot_cap)
    labels = jnp.take(local_row, pair_of_slot, axis=0, mode="clip").astype(jnp.bfloat16)
    both_axes = ("group", "dev")
    labels = labels.reshape(device_total, slot_cap)
    tags = exchange(widen(labels, feat_width), dev_count, 0)[:, :slot_cap].astype(jnp.int32)
    block_rows = 64

    def score_block(inputs):
        query_block, tag_block = inputs
        passage_block = jnp.take(passage_unit, tag_block, axis=0, mode="clip")
        logits = (
            jnp.einsum(
                "bqe,bpe->bqp", query_block, passage_block, preferred_element_type=jnp.float32
            )
            / SOFTNESS
        )
        exp_terms = jnp.exp(logits)
        token_mass = jnp.sum(exp_terms, axis=-1, keepdims=True)
        pair_score = jnp.sum(SOFTNESS * jnp.log(token_mass[..., 0]), axis=-1)
        attention = (exp_terms / token_mass).astype(jnp.bfloat16)
        pulled = jnp.einsum(
            "bqp,bpe->bqe", attention, passage_block, preferred_element_type=jnp.float32
        )
        return (pulled.astype(jnp.bfloat16), pair_score)

    returned = []
    scores = []
    pulled_parts = []
    for slot in range(slot_cap):
        outgoing = jnp.take(query_send, slot_owner[:, slot], axis=0, mode="clip")
        arrived = lax.all_to_all(outgoing, both_axes, split_axis=0, concat_axis=0, tiled=True)
        blocks = device_total // block_rows
        pulled, score = lax.map(
            score_block,
            (
                arrived.reshape(blocks, block_rows, query_len, feat_width),
                tags[:, slot].reshape(blocks, block_rows),
            ),
        )
        pulled_parts.append(pulled.reshape(device_total, query_len, feat_width))
        scores.append(score.reshape(device_total))
        if slot < slot_cap - 1:
            returned.append(
                lax.all_to_all(
                    pulled_parts[-1], both_axes, split_axis=0, concat_axis=0, tiled=True
                )
            )
    returned.append(
        lax.all_to_all(pulled_parts[-1], both_axes, split_axis=0, concat_axis=0, tiled=True)
    )
    scores = jnp.stack(scores, axis=1)
    scores_flat = exchange(widen(scores, feat_width), dev_count, 1)[:, :slot_cap]
    pair_score = jnp.take(scores_flat.reshape(slot_total), slot_index, axis=0, mode="clip").reshape(
        query_count, list_len
    )
    exp_scores = jnp.exp(pair_score)
    total = jnp.sum(exp_scores, axis=-1, keepdims=True)
    loss = jnp.log(total[:, 0]) - pair_score[:, 0]
    first = (jnp.arange(list_len) == 0).astype(jnp.float32)
    coeff = exp_scores / total - first[None, :]
    slot_of_pair = before.reshape(query_count, list_len)
    holder = target.reshape(query_count, list_len)
    holder_hit = holder[:, :, None] == jnp.arange(device_total)[None, None, :]
    unit_grad = None
    for slot in range(slot_cap):
        weight = jnp.where(slot_of_pair == slot, coeff, 0.0)
        weight = jnp.sum(jnp.where(holder_hit, weight[:, :, None], 0.0), axis=1)
        term = jnp.dot(
            weight,
            returned[slot].reshape(device_total, query_len * feat_width).astype(jnp.float32),
            precision=lax.Precision.HIGHEST,
            preferred_element_type=jnp.float32,
        ).reshape(query_count, query_len, feat_width)
        unit_grad = term if unit_grad is None else unit_grad + term
    along = jnp.sum(query_unit * unit_grad, axis=-1, keepdims=True)
    query_grad = (unit_grad - query_unit * along) * query_scale
    return (loss, query_grad)


def solution(mesh):
    placed = (
        P(("group", "dev"), None, None),
        P(("group", "dev"), None, None),
        P(("group", "dev"), None),
        P(),
    )
    return jax.shard_map(
        local,
        mesh=mesh,
        in_specs=placed,
        out_specs=(P(("group", "dev")), P(("group", "dev"), None, None)),
        check_vma=False,
    )
```

```python
import functools

import jax
import jax.numpy as jnp
from jax import lax
from jax.experimental import pallas as pl
from jax.experimental.pallas import tpu as pltpu
from jax.sharding import PartitionSpec as P

MESH = pl.DeviceIdType.MESH

SOFTNESS = 0.02
EPSILON = 1e-06


def normalize(values):
    floats = values.astype(jnp.float32)
    scale = lax.rsqrt(jnp.sum(floats * floats, axis=-1, keepdims=True) + EPSILON)
    return (floats * scale, scale)


def exchange_kernel(dev_count, rows_ref, out_ref, landing, send_sem, recv_sem):
    total = rows_ref.shape[0]
    me = lax.axis_index("group") * dev_count + lax.axis_index("dev")

    def peer_id(step):
        peer = lax.rem(me + step, total)
        return peer, (lax.div(peer, dev_count), lax.rem(peer, dev_count))

    barrier = pltpu.get_barrier_semaphore()

    def greet(step, carry):
        pl.semaphore_signal(barrier, inc=1, device_id=peer_id(step)[1], device_id_type=MESH)
        return carry

    lax.fori_loop(1, total, greet, 0)
    pl.semaphore_wait(barrier, total - 1)

    def send(step, carry):
        peer, device = peer_id(step)
        pltpu.make_async_remote_copy(
            src_ref=rows_ref.at[pl.ds(peer, 1)],
            dst_ref=landing.at[pl.ds(me, 1)],
            send_sem=send_sem,
            recv_sem=recv_sem,
            device_id=device,
            device_id_type=MESH,
        ).start()
        return carry

    lax.fori_loop(1, total, send, 0)
    landing[pl.ds(me, 1), :] = rows_ref[pl.ds(me, 1), :]
    every = pltpu.make_async_remote_copy(
        src_ref=rows_ref.at[pl.ds(0, total - 1)],
        dst_ref=landing.at[pl.ds(0, total - 1)],
        send_sem=send_sem,
        recv_sem=recv_sem,
        device_id=peer_id(1)[1],
        device_id_type=MESH,
    )
    every.wait_send()
    every.wait_recv()
    out_ref[...] = landing[...]


def exchange(rows, dev_count, tag):
    return pl.pallas_call(
        functools.partial(exchange_kernel, dev_count),
        out_shape=jax.ShapeDtypeStruct(rows.shape, rows.dtype),
        in_specs=[pl.BlockSpec(memory_space=pltpu.VMEM)],
        out_specs=pl.BlockSpec(memory_space=pltpu.VMEM),
        scratch_shapes=[
            pltpu.VMEM(rows.shape, rows.dtype),
            pltpu.SemaphoreType.DMA(()),
            pltpu.SemaphoreType.DMA(()),
        ],
        compiler_params=pltpu.CompilerParams(collective_id=tag, has_side_effects=True),
    )(rows)


def widen(small, feat_width):
    return jnp.pad(small.astype(jnp.float32), ((0, 0), (0, feat_width - small.shape[1])))


def local(queries, passages, candidates, location):
    group_count = lax.axis_size("group")
    dev_count = lax.axis_size("dev")
    device_total = group_count * dev_count
    query_count, query_len, feat_width = queries.shape
    pass_count = passages.shape[0]
    list_len = candidates.shape[1]
    pair_count = query_count * list_len
    slot_cap = max(2, (3 * pair_count + device_total - 1) // device_total)
    slot_total = device_total * slot_cap
    query_unit, query_scale = normalize(queries)
    query_send = query_unit.astype(jnp.bfloat16)
    passage_unit = normalize(passages)[0].astype(jnp.bfloat16)
    rows = jnp.take(location, candidates.reshape(-1), axis=0)
    target = rows // pass_count
    local_row = rows % pass_count
    same_target = target[:, None] == target[None, :]
    positions = jnp.arange(pair_count, dtype=jnp.int32)
    earlier = positions[None, :] < positions[:, None]
    before = jnp.sum(same_target & earlier, axis=1)
    slot_index = target * slot_cap + before
    pair_of_slot = jnp.zeros((slot_total,), jnp.int32).at[slot_index].set(positions)
    slot_owner = (pair_of_slot // list_len).reshape(device_total, slot_cap)
    labels = jnp.take(local_row, pair_of_slot, axis=0, mode="clip").astype(jnp.bfloat16)
    both_axes = ("group", "dev")
    labels = labels.reshape(device_total, slot_cap)
    tags = exchange(widen(labels, feat_width), dev_count, 0)[:, :slot_cap].astype(jnp.int32)
    tags, query_send = lax.optimization_barrier((tags, query_send))
    block_rows = 64

    def score_block(inputs):
        query_block, tag_block = inputs
        passage_block = jnp.take(passage_unit, tag_block, axis=0, mode="clip")
        logits = (
            jnp.einsum(
                "bqe,bpe->bqp", query_block, passage_block, preferred_element_type=jnp.float32
            )
            / SOFTNESS
        )
        exp_terms = jnp.exp(logits)
        token_mass = jnp.sum(exp_terms, axis=-1, keepdims=True)
        pair_score = jnp.sum(SOFTNESS * jnp.log(token_mass[..., 0]), axis=-1)
        attention = (exp_terms / token_mass).astype(jnp.bfloat16)
        pulled = jnp.einsum(
            "bqp,bpe->bqe", attention, passage_block, preferred_element_type=jnp.float32
        )
        return (pulled.astype(jnp.bfloat16), pair_score)

    returned = []
    scores = []
    pulled_parts = []
    for slot in range(slot_cap):
        outgoing = jnp.take(query_send, slot_owner[:, slot], axis=0, mode="clip")
        arrived = lax.all_to_all(outgoing, both_axes, split_axis=0, concat_axis=0, tiled=True)
        blocks = device_total // block_rows
        pulled, score = lax.map(
            score_block,
            (
                arrived.reshape(blocks, block_rows, query_len, feat_width),
                tags[:, slot].reshape(blocks, block_rows),
            ),
        )
        pulled_parts.append(pulled.reshape(device_total, query_len, feat_width))
        scores.append(score.reshape(device_total))
        if slot < slot_cap - 1:
            returned.append(
                lax.all_to_all(
                    pulled_parts[-1], both_axes, split_axis=0, concat_axis=0, tiled=True
                )
            )
    returned.append(
        lax.all_to_all(pulled_parts[-1], both_axes, split_axis=0, concat_axis=0, tiled=True)
    )
    scores = jnp.stack(scores, axis=1)
    scores_flat = exchange(widen(scores, feat_width), dev_count, 1)[:, :slot_cap]
    pair_score = jnp.take(scores_flat.reshape(slot_total), slot_index, axis=0, mode="clip").reshape(
        query_count, list_len
    )
    exp_scores = jnp.exp(pair_score)
    total = jnp.sum(exp_scores, axis=-1, keepdims=True)
    loss = jnp.log(total[:, 0]) - pair_score[:, 0]
    first = (jnp.arange(list_len) == 0).astype(jnp.float32)
    coeff = exp_scores / total - first[None, :]
    slot_of_pair = before.reshape(query_count, list_len)
    unit_grad = None
    for slot in range(slot_cap):
        part = jnp.take(returned[slot], target, axis=0, mode="clip").reshape(
            query_count, list_len, query_len, feat_width
        )
        weight = jnp.where(slot_of_pair == slot, coeff, 0.0)
        term = jnp.einsum("bk,bkqe->bqe", weight, part.astype(jnp.float32))
        unit_grad = term if unit_grad is None else unit_grad + term
    along = jnp.sum(query_unit * unit_grad, axis=-1, keepdims=True)
    query_grad = (unit_grad - query_unit * along) * query_scale
    return (loss, query_grad)


def solution(mesh):
    placed = (
        P(("group", "dev"), None, None),
        P(("group", "dev"), None, None),
        P(("group", "dev"), None),
        P(),
    )
    return jax.shard_map(
        local,
        mesh=mesh,
        in_specs=placed,
        out_specs=(P(("group", "dev")), P(("group", "dev"), None, None)),
        check_vma=False,
    )
```

```python
import functools

import jax
import jax.numpy as jnp
from jax import lax
from jax.experimental import pallas as pl
from jax.experimental.pallas import tpu as pltpu
from jax.sharding import PartitionSpec as P

MESH = pl.DeviceIdType.MESH

SOFTNESS = 0.02
EPSILON = 1e-06


def normalize(values):
    floats = values.astype(jnp.float32)
    scale = lax.rsqrt(jnp.sum(floats * floats, axis=-1, keepdims=True) + EPSILON)
    return (floats * scale, scale)


def exchange_kernel(dev_count, rows_ref, out_ref, landing, send_sem, recv_sem):
    total = rows_ref.shape[0]
    me = lax.axis_index("group") * dev_count + lax.axis_index("dev")

    def peer_id(step):
        peer = lax.rem(me + step, total)
        return peer, (lax.div(peer, dev_count), lax.rem(peer, dev_count))

    barrier = pltpu.get_barrier_semaphore()

    def greet(step, carry):
        pl.semaphore_signal(barrier, inc=1, device_id=peer_id(step)[1], device_id_type=MESH)
        return carry

    lax.fori_loop(1, total, greet, 0)
    pl.semaphore_wait(barrier, total - 1)

    def send(step, carry):
        peer, device = peer_id(step)
        pltpu.make_async_remote_copy(
            src_ref=rows_ref.at[pl.ds(peer, 1)],
            dst_ref=landing.at[pl.ds(me, 1)],
            send_sem=send_sem,
            recv_sem=recv_sem,
            device_id=device,
            device_id_type=MESH,
        ).start()
        return carry

    lax.fori_loop(1, total, send, 0)
    landing[pl.ds(me, 1), :] = rows_ref[pl.ds(me, 1), :]
    every = pltpu.make_async_remote_copy(
        src_ref=rows_ref.at[pl.ds(0, total - 1)],
        dst_ref=landing.at[pl.ds(0, total - 1)],
        send_sem=send_sem,
        recv_sem=recv_sem,
        device_id=peer_id(1)[1],
        device_id_type=MESH,
    )
    every.wait_send()
    every.wait_recv()
    out_ref[...] = landing[...]


def exchange(rows, dev_count, tag):
    return pl.pallas_call(
        functools.partial(exchange_kernel, dev_count),
        out_shape=jax.ShapeDtypeStruct(rows.shape, rows.dtype),
        in_specs=[pl.BlockSpec(memory_space=pltpu.VMEM)],
        out_specs=pl.BlockSpec(memory_space=pltpu.VMEM),
        scratch_shapes=[
            pltpu.VMEM(rows.shape, rows.dtype),
            pltpu.SemaphoreType.DMA(()),
            pltpu.SemaphoreType.DMA(()),
        ],
        compiler_params=pltpu.CompilerParams(collective_id=tag, has_side_effects=True),
    )(rows)


def widen(small, feat_width):
    return jnp.pad(small.astype(jnp.float32), ((0, 0), (0, feat_width - small.shape[1])))


def local(queries, passages, candidates, location):
    group_count = lax.axis_size("group")
    dev_count = lax.axis_size("dev")
    device_total = group_count * dev_count
    query_count, query_len, feat_width = queries.shape
    pass_count = passages.shape[0]
    list_len = candidates.shape[1]
    pair_count = query_count * list_len
    slot_cap = max(2, (3 * pair_count + device_total - 1) // device_total)
    slot_total = device_total * slot_cap
    query_unit, query_scale = normalize(queries)
    query_send = query_unit.astype(jnp.bfloat16)
    passage_unit = normalize(passages)[0].astype(jnp.bfloat16)
    rows = jnp.take(location, candidates.reshape(-1), axis=0)
    target = rows // pass_count
    local_row = rows % pass_count
    same_target = target[:, None] == target[None, :]
    positions = jnp.arange(pair_count, dtype=jnp.int32)
    earlier = positions[None, :] < positions[:, None]
    before = jnp.sum(same_target & earlier, axis=1)
    slot_index = target * slot_cap + before
    pair_of_slot = jnp.zeros((slot_total,), jnp.int32).at[slot_index].set(positions)
    slot_owner = (pair_of_slot // list_len).reshape(device_total, slot_cap)
    labels = jnp.take(local_row, pair_of_slot, axis=0, mode="clip").astype(jnp.bfloat16)
    both_axes = ("group", "dev")
    labels = labels.reshape(device_total, slot_cap)
    tags = exchange(widen(labels, feat_width), dev_count, 0)[:, :slot_cap].astype(jnp.int32)
    block_rows = 64

    def score_block(inputs):
        query_block, tag_block = inputs
        passage_block = jnp.take(passage_unit, tag_block, axis=0, mode="clip")
        logits = (
            jnp.einsum(
                "bqe,bpe->bqp", query_block, passage_block, preferred_element_type=jnp.float32
            )
            / SOFTNESS
        )
        exp_terms = jnp.exp(logits)
        token_mass = jnp.sum(exp_terms, axis=-1, keepdims=True)
        pair_score = jnp.sum(SOFTNESS * jnp.log(token_mass[..., 0]), axis=-1)
        attention = (exp_terms / token_mass).astype(jnp.bfloat16)
        pulled = jnp.einsum(
            "bqp,bpe->bqe", attention, passage_block, preferred_element_type=jnp.float32
        )
        return (pulled.astype(jnp.bfloat16), pair_score)

    returned = []
    scores = []
    pulled_parts = []
    for slot in range(slot_cap):
        outgoing = jnp.take(query_send, slot_owner[:, slot], axis=0, mode="clip")
        arrived = lax.all_to_all(outgoing, both_axes, split_axis=0, concat_axis=0, tiled=True)
        blocks = device_total // block_rows
        pulled, score = lax.map(
            score_block,
            (
                arrived.reshape(blocks, block_rows, query_len, feat_width),
                tags[:, slot].reshape(blocks, block_rows),
            ),
        )
        pulled_parts.append(pulled.reshape(device_total, query_len, feat_width))
        scores.append(score.reshape(device_total))
        if slot < slot_cap - 1:
            returned.append(
                lax.all_to_all(
                    pulled_parts[-1], both_axes, split_axis=0, concat_axis=0, tiled=True
                )
            )
    returned.append(
        lax.all_to_all(pulled_parts[-1], both_axes, split_axis=0, concat_axis=0, tiled=True)
    )
    scores = jnp.stack(scores, axis=1)
    scores_flat = exchange(widen(scores, feat_width), dev_count, 1)[:, :slot_cap]
    pair_score = jnp.take(scores_flat[:, 0], target, axis=0, mode="clip")
    for slot in range(1, slot_cap):
        pair_score = jnp.where(
            before == slot, jnp.take(scores_flat[:, slot], target, axis=0, mode="clip"), pair_score
        )
    pair_score = pair_score.reshape(query_count, list_len)
    exp_scores = jnp.exp(pair_score)
    total = jnp.sum(exp_scores, axis=-1, keepdims=True)
    loss = jnp.log(total[:, 0]) - pair_score[:, 0]
    first = (jnp.arange(list_len) == 0).astype(jnp.float32)
    coeff = exp_scores / total - first[None, :]
    slot_of_pair = before.reshape(query_count, list_len)
    unit_grad = None
    for slot in range(slot_cap):
        part = jnp.take(returned[slot], target, axis=0, mode="clip").reshape(
            query_count, list_len, query_len, feat_width
        )
        weight = jnp.where(slot_of_pair == slot, coeff, 0.0)
        term = jnp.einsum("bk,bkqe->bqe", weight, part.astype(jnp.float32))
        unit_grad = term if unit_grad is None else unit_grad + term
    along = jnp.sum(query_unit * unit_grad, axis=-1, keepdims=True)
    query_grad = (unit_grad - query_unit * along) * query_scale
    return (loss, query_grad)


def solution(mesh):
    placed = (
        P(("group", "dev"), None, None),
        P(("group", "dev"), None, None),
        P(("group", "dev"), None),
        P(),
    )
    return jax.shard_map(
        local,
        mesh=mesh,
        in_specs=placed,
        out_specs=(P(("group", "dev")), P(("group", "dev"), None, None)),
        check_vma=False,
    )
```

```python
import functools

import jax
import jax.numpy as jnp
from jax import lax
from jax.experimental import pallas as pl
from jax.experimental.pallas import tpu as pltpu
from jax.sharding import PartitionSpec as P

MESH = pl.DeviceIdType.MESH

SOFTNESS = 0.02
EPSILON = 1e-06


def normalize(values):
    floats = values.astype(jnp.float32)
    scale = lax.rsqrt(jnp.sum(floats * floats, axis=-1, keepdims=True) + EPSILON)
    return (floats * scale, scale)


def exchange_kernel(dev_count, rows_ref, out_ref, landing, send_sem, recv_sem):
    total = rows_ref.shape[0]
    me = lax.axis_index("group") * dev_count + lax.axis_index("dev")

    def peer_id(step):
        peer = lax.rem(me + step, total)
        return peer, (lax.div(peer, dev_count), lax.rem(peer, dev_count))

    barrier = pltpu.get_barrier_semaphore()

    def greet(step, carry):
        pl.semaphore_signal(barrier, inc=1, device_id=peer_id(step)[1], device_id_type=MESH)
        return carry

    lax.fori_loop(1, total, greet, 0)
    pl.semaphore_wait(barrier, total - 1)

    def send(step, carry):
        peer, device = peer_id(step)
        pltpu.make_async_remote_copy(
            src_ref=rows_ref.at[pl.ds(peer, 1)],
            dst_ref=landing.at[pl.ds(me, 1)],
            send_sem=send_sem,
            recv_sem=recv_sem,
            device_id=device,
            device_id_type=MESH,
        ).start()
        return carry

    lax.fori_loop(1, total, send, 0)
    landing[pl.ds(me, 1), :] = rows_ref[pl.ds(me, 1), :]
    every = pltpu.make_async_remote_copy(
        src_ref=rows_ref.at[pl.ds(0, total - 1)],
        dst_ref=landing.at[pl.ds(0, total - 1)],
        send_sem=send_sem,
        recv_sem=recv_sem,
        device_id=peer_id(1)[1],
        device_id_type=MESH,
    )
    every.wait_send()
    every.wait_recv()
    out_ref[...] = landing[...]


def exchange(rows, dev_count, tag):
    return pl.pallas_call(
        functools.partial(exchange_kernel, dev_count),
        out_shape=jax.ShapeDtypeStruct(rows.shape, rows.dtype),
        in_specs=[pl.BlockSpec(memory_space=pltpu.VMEM)],
        out_specs=pl.BlockSpec(memory_space=pltpu.VMEM),
        scratch_shapes=[
            pltpu.VMEM(rows.shape, rows.dtype),
            pltpu.SemaphoreType.DMA(()),
            pltpu.SemaphoreType.DMA(()),
        ],
        compiler_params=pltpu.CompilerParams(collective_id=tag, has_side_effects=True),
    )(rows)


def widen(small, feat_width):
    return jnp.pad(small.astype(jnp.float32), ((0, 0), (0, feat_width - small.shape[1])))


def local(queries, passages, candidates, location):
    group_count = lax.axis_size("group")
    dev_count = lax.axis_size("dev")
    device_total = group_count * dev_count
    query_count, query_len, feat_width = queries.shape
    pass_count = passages.shape[0]
    list_len = candidates.shape[1]
    pair_count = query_count * list_len
    slot_cap = max(2, (3 * pair_count + device_total - 1) // device_total)
    slot_total = device_total * slot_cap
    query_unit, query_scale = normalize(queries)
    query_send = query_unit.astype(jnp.bfloat16)
    passage_unit = normalize(passages)[0].astype(jnp.bfloat16)
    rows = jnp.take(location, candidates.reshape(-1), axis=0)
    target = rows // pass_count
    local_row = rows % pass_count
    same_target = target[:, None] == target[None, :]
    positions = jnp.arange(pair_count, dtype=jnp.int32)
    earlier = positions[None, :] < positions[:, None]
    before = jnp.sum(same_target & earlier, axis=1)
    slot_index = target * slot_cap + before
    pair_of_slot = jnp.zeros((slot_total,), jnp.int32).at[slot_index].set(positions)
    slot_owner = (pair_of_slot // list_len).reshape(device_total, slot_cap)
    labels = jnp.take(local_row, pair_of_slot, axis=0, mode="clip").astype(jnp.bfloat16)
    both_axes = ("group", "dev")
    labels = labels.reshape(device_total, slot_cap)
    tags = exchange(labels.astype(jnp.float32), dev_count, 0).astype(jnp.int32)
    block_rows = 64

    def score_block(inputs):
        query_block, tag_block = inputs
        passage_block = jnp.take(passage_unit, tag_block, axis=0, mode="clip")
        logits = (
            jnp.einsum(
                "bqe,bpe->bqp", query_block, passage_block, preferred_element_type=jnp.float32
            )
            / SOFTNESS
        )
        exp_terms = jnp.exp(logits)
        token_mass = jnp.sum(exp_terms, axis=-1, keepdims=True)
        pair_score = jnp.sum(SOFTNESS * jnp.log(token_mass[..., 0]), axis=-1)
        attention = (exp_terms / token_mass).astype(jnp.bfloat16)
        pulled = jnp.einsum(
            "bqp,bpe->bqe", attention, passage_block, preferred_element_type=jnp.float32
        )
        return (pulled.astype(jnp.bfloat16), pair_score)

    returned = []
    scores = []
    pulled_parts = []
    for slot in range(slot_cap):
        outgoing = jnp.take(query_send, slot_owner[:, slot], axis=0, mode="clip")
        arrived = lax.all_to_all(outgoing, both_axes, split_axis=0, concat_axis=0, tiled=True)
        blocks = device_total // block_rows
        pulled, score = lax.map(
            score_block,
            (
                arrived.reshape(blocks, block_rows, query_len, feat_width),
                tags[:, slot].reshape(blocks, block_rows),
            ),
        )
        pulled_parts.append(pulled.reshape(device_total, query_len, feat_width))
        scores.append(score.reshape(device_total))
        if slot < slot_cap - 1:
            returned.append(
                lax.all_to_all(
                    pulled_parts[-1], both_axes, split_axis=0, concat_axis=0, tiled=True
                )
            )
    returned.append(
        lax.all_to_all(pulled_parts[-1], both_axes, split_axis=0, concat_axis=0, tiled=True)
    )
    scores = jnp.stack(scores, axis=1)
    scores_flat = exchange(scores, dev_count, 1)
    pair_score = jnp.take(scores_flat.reshape(slot_total), slot_index, axis=0, mode="clip").reshape(
        query_count, list_len
    )
    exp_scores = jnp.exp(pair_score)
    total = jnp.sum(exp_scores, axis=-1, keepdims=True)
    loss = jnp.log(total[:, 0]) - pair_score[:, 0]
    first = (jnp.arange(list_len) == 0).astype(jnp.float32)
    coeff = exp_scores / total - first[None, :]
    slot_of_pair = before.reshape(query_count, list_len)
    unit_grad = None
    for slot in range(slot_cap):
        part = jnp.take(returned[slot], target, axis=0, mode="clip").reshape(
            query_count, list_len, query_len, feat_width
        )
        weight = jnp.where(slot_of_pair == slot, coeff, 0.0)
        term = jnp.einsum("bk,bkqe->bqe", weight, part.astype(jnp.float32))
        unit_grad = term if unit_grad is None else unit_grad + term
    along = jnp.sum(query_unit * unit_grad, axis=-1, keepdims=True)
    query_grad = (unit_grad - query_unit * along) * query_scale
    return (loss, query_grad)


def solution(mesh):
    placed = (
        P(("group", "dev"), None, None),
        P(("group", "dev"), None, None),
        P(("group", "dev"), None),
        P(),
    )
    return jax.shard_map(
        local,
        mesh=mesh,
        in_specs=placed,
        out_specs=(P(("group", "dev")), P(("group", "dev"), None, None)),
        check_vma=False,
    )
```
